128 devices in a mesh: dp: 16 (over y_lo, z, core), zero: 8 (over y_hi, x).
Axes of the slice: x: 4, y: 4 (y_hi: 2, y_lo: 2; y = y_hi * 2 + y_lo), z: 4, core: 2. Of those that a mesh axis runs over, the one named last changes fastest.
Arguments:
- query_rows: bfloat16 [114688, 2048], P(('dp', 'zero')), may hold values from -40 to 40
- key_rows: bfloat16 [114688, 512], P(('dp', 'zero')), may hold values from -6 to 6
- value_rows: bfloat16 [114688, 512], P(('dp', 'zero')), may hold values from -6 to 6
- output_grad: bfloat16 [114688, 2048], P(('dp', 'zero')), may hold values from -6 to 6
- home_lengths: int32 [128, 6], P(('dp', 'zero')), may hold values from 1 to 96, 384 in all within a row
- moved_lengths: int32 [128, 8], P(('dp', 'zero')), may hold values from 48 to 64, as said below
- moved_offsets: int32 [128, 8], P(('dp', 'zero')), may hold values from 0 to 448, as said below
- moved_owner: int32 [128, 8], P(('dp', 'zero')), may hold values from 0 to 15, as said below
- owner_offsets: int32 [128, 8], P(('dp', 'zero')), may hold values from 0 to 448, as said below
- layer_grad: bfloat16 [16, 8, 4096, 512], P('dp', 'zero'), may hold values from -0.59765625 to 0.59765625
Outputs:
- attention: bfloat16 [114688, 2048], P(('dp', 'zero'))
- query_grad: bfloat16 [114688, 2048], P(('dp', 'zero'))
- key_grad: bfloat16 [114688, 512], P(('dp', 'zero'))
- value_grad: bfloat16 [114688, 512], P(('dp', 'zero'))
- summed_grad: float32 [4096, 512], P('zero')
The draws below stay inside these ranges and needn't reach their ends.
Inputs may be any that keep to these rules, and one draw needn't show every extreme that they name: `moved_lengths`: every device moves exactly 8 documents, laid end to end in its last 512 rows. `moved_offsets`: each moved document starts where the one before it ends; the first starts at 0. `moved_owner`: A receiver keeps the sender's zero index. The 8 documents of one device go to 8 different dp indices, and every device receives exactly 8 documents. `owner_offsets`: the documents that a device receives lie end to end from the start of its last 512 rows, in all at most 512 rows; in every draw some device receives exactly 512 rows. `home_lengths`: each device's home documents fill its first 384 rows.
All inputs are finite; a program needn't handle non-finite values.
Results may differ from the reference program's by a relative error of at most 0.013.
Values may be sent and summed in bfloat16 or wider, within the bound.
No kernel may reach another device: no remote copies, remote signals or barrier semaphores. Data moves between devices by JAX's collectives and lax.ppermute only.
A program may use at most 128 MiB of HBM per device.

```python
import math
import jax
import jax.numpy as jnp
import numpy as np
from jax import lax

D = 4096
HD = 128
H = 16
KV = 4
HOME = 384
NHOME = 6
S = 64
NMOV = 8
HMAX = 96
MOVE = 512
TOK_DEV = 896
ROWS = 114688
N_DP = 16
N_ZERO = 8


def moved_plan(key):
    base_key = jax.random.fold_in(key, 101)
    first_key, second_key, third_key = jax.random.split(base_key, 3)
    ranking = jax.random.randint(first_key, (N_ZERO, N_DP), 0, 1 << 20) * N_DP + jnp.arange(N_DP, dtype=jnp.int32)[None, :]
    shifts = lax.top_k(ranking, NMOV)[1].astype(jnp.int32)
    chosen = jax.random.randint(second_key, (N_ZERO,), 0, N_DP).astype(jnp.int32)
    lengths = jax.random.randint(third_key, (N_DP, N_ZERO, NMOV), S - S // 4, S + 1).astype(jnp.int32)
    senders = (chosen[:, None] - shifts) % N_DP
    ranks = jnp.arange(N_DP, dtype=jnp.int32)[:, None, None]
    lengths = jnp.where(ranks == senders[None], S, lengths).astype(jnp.int32)
    lengths = jnp.where(ranks == 0, S, lengths).astype(jnp.int32)
    owners = ((ranks + shifts[None]) % N_DP).astype(jnp.int32)
    offsets = (jnp.cumsum(lengths, axis=2) - lengths).astype(jnp.int32)
    incoming_from = ((ranks - shifts[None]) % N_DP).astype(jnp.int32)
    incoming = jnp.take_along_axis(lengths, incoming_from, axis=0)
    landing_all = (jnp.cumsum(incoming, axis=2) - incoming).astype(jnp.int32)
    landing = jnp.take_along_axis(landing_all, owners, axis=0).astype(jnp.int32)
    flat_rows = N_DP * N_ZERO
    return (lengths.reshape(flat_rows, NMOV), offsets.reshape(flat_rows, NMOV), owners.reshape(flat_rows, NMOV), landing.reshape(flat_rows, NMOV))


def draw_moved_lengths(key, part):
    return moved_plan(key)[0]


def draw_moved_offsets(key, part):
    return moved_plan(key)[1]


def draw_moved_owner(key, part):
    return moved_plan(key)[2]


def draw_owner_offsets(key, part):
    return moved_plan(key)[3]


def key_field(key):
    base_key = jax.random.fold_in(key, 202)
    shape_keys = (ROWS, KV * HD)
    field = jnp.clip(jax.random.normal(base_key, shape_keys, jnp.float32), -6.0, 6.0)
    return field


def draw_key_rows(key, part):
    return key_field(key).astype(jnp.bfloat16)


def draw_query_rows(key, part):
    base_key = jax.random.fold_in(key, 303)
    shape_queries = (ROWS, H * HD)
    field = jnp.clip(jax.random.normal(base_key, shape_queries, jnp.float32), -6.0, 6.0)
    return field.astype(jnp.bfloat16)


def raised(drawn, rng, source, target, blocks, factor):
    owner, partner = [(jnp.arange(drawn.shape[dim]) // (drawn.shape[dim] // blocks)).reshape([-1 if axis == dim else 1 for axis in range(drawn.ndim)]) for dim in (source, target)]
    chosen = jax.random.permutation(rng, blocks)[partner]
    strong = (owner == chosen) | (owner == (partner + blocks // 2) % blocks)
    return jnp.where(strong, factor * drawn, drawn)


def block_scale(own_key, shape, cuts, least, high):
    factor_of, own = 1.0, jax.random.fold_in(own_key, 6)
    for axis_at, parts in cuts:
        draws = jnp.exp(jax.random.uniform(jax.random.fold_in(own, axis_at), (parts,), jnp.float32, least / len(cuts), high / len(cuts)))
        factor_of = factor_of * jnp.repeat(draws, shape[axis_at] // parts).reshape([-1 if axis == axis_at else 1 for axis in range(len(shape))])
    return factor_of


def length_profile(amount, total, most, skew):
    weights = [(1 << 20) // math.isqrt(standing ** skew) + 1 for standing in range(2, amount + 1)]
    rest, holding = total - most - (amount - 1), [1] * (amount - 1)
    while rest > 0:
        candidates = [i for i in range(amount - 1) if holding[i] < most]
        whole, budget = sum([weights[i] for i in candidates]), rest
        for i in candidates:
            more = min(most - holding[i], max(1, budget * weights[i] // whole), rest)
            holding[i] = holding[i] + more
            rest = rest - more
    return np.array([most] + holding)


def ragged(own_key, number_of, total, most, slope):
    if number_of == 2:
        one = jax.random.randint(own_key, (), max(1, total - most), min(most, total - 1) + 1)
        return jnp.stack([one, total - one])
    sizes = jnp.asarray(length_profile(number_of, total, most, slope), jnp.int32)
    twos = (number_of - 1) // 2
    giver, taker = sizes[1:1 + 2 * twos:2], sizes[2:2 + 2 * twos:2]
    room = jnp.minimum(giver - 1, most - taker)
    shifted = jax.random.randint(jax.random.fold_in(own_key, 1), (twos,), 0, 1 << 20) % (room + 1)
    sizes = sizes.at[1:1 + 2 * twos:2].set(giver - shifted).at[2:2 + 2 * twos:2].set(taker + shifted)
    return sizes[jax.random.permutation(jax.random.fold_in(own_key, 2), number_of)]


def normal_values(stream_key, dims, spread, limit, cuts=(), kind=jnp.bfloat16):
    gain = block_scale(stream_key, dims, cuts, -0.22, 0.18) if cuts else 1.0
    entries = jax.random.normal(stream_key, dims, jnp.float32) * spread * gain
    return jnp.minimum(jnp.maximum(entries, -limit), limit).astype(kind)


def bell_draw_with(key, extent, scale, reach, shards, heavy, held_as=jnp.bfloat16):
    entries = scale * jax.random.normal(key, extent, jnp.float32)
    if shards:
        entries = entries * block_scale(key, extent, shards, -0.22, 0.18)
    return jnp.clip(raised(entries, jax.random.fold_in(key, 3), *heavy), -reach, reach).astype(held_as)


def setup_inputs(seed: int = 0) -> dict:
    seeds = jax.random.split(jax.random.key(seed), 11)
    query_rows = draw_query_rows(jax.random.fold_in(seeds[10], 71), 0)
    key_rows = draw_key_rows(jax.random.fold_in(seeds[10], 71), 0)
    value_rows = normal_values(seeds[2], (ROWS, KV * HD), 1.0, 6.0, ((0, 128),))
    output_grad = normal_values(seeds[3], (ROWS, H * HD), 1.0, 6.0, ((0, 128),))
    home_lengths = jax.vmap(lambda own: ragged(own, NHOME, HOME, HOME // 4, 1))(jax.random.split(seeds[4], (N_DP * N_ZERO))).reshape((N_DP * N_ZERO, NHOME)).astype(jnp.int32)
    moved_lengths = draw_moved_lengths(jax.random.fold_in(seeds[10], 71), 0)
    moved_offsets = draw_moved_offsets(jax.random.fold_in(seeds[10], 71), 0)
    moved_owner = draw_moved_owner(jax.random.fold_in(seeds[10], 71), 0)
    owner_offsets = draw_owner_offsets(jax.random.fold_in(seeds[10], 71), 0)
    layer_grad = bell_draw_with(seeds[9], (N_DP, N_ZERO, D, KV * HD), 0.1, 0.59765625, ((0, 16), (1, 8)), (1, 2, 8, 2.0))
    return {"query_rows": query_rows, "key_rows": key_rows, "value_rows": value_rows, "output_grad": output_grad, "home_lengths": home_lengths, "moved_lengths": moved_lengths, "moved_offsets": moved_offsets, "moved_owner": moved_owner, "owner_offsets": owner_offsets, "layer_grad": layer_grad}


def attend(query_matrix, keys_in, values_in, grads_in, documents):
    length = query_matrix.shape[0]
    kv_heads = keys_in.shape[1] // HD
    per_group = query_matrix.shape[1] // keys_in.shape[1]
    softmax_scale = 1.0 / math.sqrt(HD)
    query_f = query_matrix.astype(jnp.float32).reshape(length, kv_heads, per_group, HD)
    key_f = keys_in.astype(jnp.float32).reshape(length, kv_heads, HD)
    value_f = values_in.astype(jnp.float32).reshape(length, kv_heads, HD)
    grad_f = grads_in.astype(jnp.float32).reshape(length, kv_heads, per_group, HD)
    position = jnp.arange(length, dtype=jnp.int32)
    allowed = (documents[:, None] == documents[None, :]) & (position[None, :] <= position[:, None])
    scores = jnp.einsum('rcgd,tcd->cgrt', query_f, key_f) * softmax_scale
    scores = jnp.where(allowed[None, None], scores, -jnp.inf)
    highest = lax.optimization_barrier(jnp.max(scores, axis=-1, keepdims=True))
    exponent = jnp.exp(scores - highest)
    weights = exponent / lax.optimization_barrier(jnp.sum(exponent, axis=-1, keepdims=True))
    weights_f = lax.optimization_barrier(weights.astype(jnp.bfloat16)).astype(jnp.float32)
    attention = jnp.einsum('cgrt,tcd->rcgd', weights_f, value_f).astype(jnp.bfloat16)
    attention_f = lax.optimization_barrier(attention).astype(jnp.float32)
    value_grad = jnp.einsum('cgrt,rcgd->tcd', weights_f, grad_f).astype(jnp.bfloat16)
    logit_matrix = jnp.einsum('rcgd,tcd->cgrt', grad_f, value_f)
    row_delta = jnp.einsum('rcgd,rcgd->cgr', grad_f, attention_f)
    score_gradient = (weights * (logit_matrix - row_delta[..., None])).astype(jnp.bfloat16)
    scores_f = lax.optimization_barrier(score_gradient).astype(jnp.float32)
    query_grad = (jnp.einsum('cgrt,tcd->rcgd', scores_f, key_f) * softmax_scale).astype(jnp.bfloat16)
    key_grad = (jnp.einsum('cgrt,rcgd->tcd', scores_f, query_f) * softmax_scale).astype(jnp.bfloat16)
    return (attention.reshape(length, -1), query_grad.reshape(length, -1), key_grad.reshape(length, -1), value_grad.reshape(length, -1))

def reference(query_rows, key_rows, value_rows, output_grad, home_lengths, moved_lengths, moved_offsets, moved_owner, owner_offsets, layer_grad):
    devices = N_DP * N_ZERO
    margin = HMAX + S

    def one_device(device):
        first_row = (device * TOK_DEV).astype(jnp.int32)
        padded = tuple((jnp.concatenate([lax.dynamic_slice_in_dim(source, first_row, TOK_DEV, 0), jnp.zeros((margin, source.shape[1]), source.dtype)], axis=0) for source in (query_rows, key_rows, value_rows, output_grad)))
        lengths = home_lengths[device]
        starts = (jnp.cumsum(lengths) - lengths).astype(jnp.int32)

        def home_doc(doc_start, doc_length):
            pieces = tuple((lax.dynamic_slice_in_dim(source, doc_start.astype(jnp.int32), HMAX, 0) for source in padded))
            position = jnp.arange(HMAX, dtype=jnp.int32)
            documents = jnp.where(position < doc_length, 0, -1).astype(jnp.int32)
            target = jnp.where(position < doc_length, doc_start + position, HOME).astype(jnp.int32)
            return (attend(pieces[0], pieces[1], pieces[2], pieces[3], documents), target)
        results, targets = jax.vmap(home_doc)(starts, lengths)
        home = tuple((jnp.zeros((HOME, result.shape[-1]), jnp.bfloat16).at[targets.reshape(-1)].set(result.reshape(-1, result.shape[-1]), mode='drop') for result in results))

        def moved_doc(doc_start, doc_length, owner_dp, landing):
            pieces = tuple((lax.dynamic_slice_in_dim(source, (HOME + doc_start).astype(jnp.int32), S, 0) for source in padded))
            position = jnp.arange(S, dtype=jnp.int32)
            documents = jnp.where(position < doc_length, 0, -1).astype(jnp.int32)
            receiver = owner_dp * N_ZERO + device % N_ZERO
            target = jnp.where(position < doc_length, receiver * TOK_DEV + HOME + landing + position, ROWS).astype(jnp.int32)
            return (attend(pieces[0], pieces[1], pieces[2], pieces[3], documents), target)
        moved, moved_targets = jax.vmap(moved_doc)(moved_offsets[device], moved_lengths[device], moved_owner[device], owner_offsets[device])
        return (home, moved, moved_targets)
    home, moved, targets = lax.map(one_device, jnp.arange(devices, dtype=jnp.int32))
    outputs = []
    for home_part, moved_part in zip(home, moved):
        columns = home_part.shape[-1]
        assembled = jnp.concatenate([home_part, jnp.zeros((devices, MOVE, columns), jnp.bfloat16)], axis=1).reshape(ROWS, columns)
        outputs.append(assembled.at[targets.reshape(-1)].set(moved_part.reshape(-1, columns), mode='drop'))
    summed_grad = lax.optimization_barrier(jnp.sum(layer_grad.astype(jnp.float32), axis=(0, 1)))
    return (outputs[0], outputs[1], outputs[2], outputs[3], summed_grad)
```

```python
import functools
import math

import jax
import jax.numpy as jnp
from jax import lax
from jax.experimental import pallas as pl
from jax.experimental.pallas import tpu as pltpu
from jax.sharding import Mesh
from jax.sharding import PartitionSpec as P

HD = 128
HOME = 384
S = 64
MOVE = 512
NDOC = 8
GROUP = 4
KV = 4
WIN = 80
NSLOT = 16
KVROWS = 6 * S
META = 8
SCALE = 1.0 / math.sqrt(HD)
EXP2_SCALE = SCALE * math.log2(math.e)
FINE = ("ylo", "z", "core", "yhi", "x")
DP = ("ylo", "z", "core")
BF = jnp.bfloat16
F32 = jnp.float32


def dot(a, b, dims):
    return lax.dot_general(a, b, (dims, ((), ())), preferred_element_type=F32)


NN = ((1,), (0,))
NT = ((1,), (1,))
TN = ((0,), (0,))


def heads_to_rows(x):
    return jnp.concatenate([x[:, HD * h : HD * (h + 1)] for h in range(GROUP)], axis=0)


def transposed_softmax(scores, allowed):
    scores = jnp.where(allowed, scores * EXP2_SCALE, -1e30)
    highest = jnp.max(scores, axis=0, keepdims=True)
    exponent = jnp.where(allowed, jnp.exp2(scores - highest), 0.0)
    total = jnp.sum(exponent, axis=0, keepdims=True)
    return exponent * (1.0 / jnp.maximum(total, 1e-30))


def send_kernel(kvs, with_meta, table, q_hbm, k_hbm, v_hbm, g_hbm, out_hbm, q, k, v, g, slot, meta, in_sem, out_sem, meta_sem):
    c0, nc = kvs[0], len(kvs)
    wide, narrow = pl.ds(GROUP * HD * c0, GROUP * HD * nc), pl.ds(HD * c0, HD * nc)
    rows = pl.ds(HOME, MOVE)
    loads = [
        pltpu.make_async_copy(k_hbm.at[rows, narrow], k, in_sem.at[0]),
        pltpu.make_async_copy(v_hbm.at[rows, narrow], v, in_sem.at[1]),
        pltpu.make_async_copy(q_hbm.at[rows, wide], q, in_sem.at[2]),
        pltpu.make_async_copy(g_hbm.at[rows, wide], g, in_sem.at[3]),
    ]
    for load in loads:
        load.start()
    if with_meta:
        lane = lax.broadcasted_iota(jnp.int32, (META, HD), 1)
        for s in range(NSLOT):
            code = jnp.int32(0)
            for d in range(NDOC):
                code = code + jnp.where(table[2, d] == s, table[3, d] + 1, 0)
            high = lax.shift_right_logical(code, 5)
            meta[s] = jnp.where(lane < S, high, code & 31).astype(F32).astype(BF)
        meta_copy = pltpu.make_async_copy(meta, out_hbm.at[:, pl.ds(KVROWS * nc, META), :], meta_sem)
        meta_copy.start()
    for load in loads:
        load.wait()

    def store(d):
        return pltpu.make_async_copy(slot.at[d % 2], out_hbm.at[table[2, d], pl.ds(0, KVROWS * nc), :], out_sem.at[d % 2])

    for d in range(NDOC):
        length, offset, landing = table[0, d], table[1, d], table[3, d]
        start = pl.multiple_of(jnp.minimum(lax.shift_right_logical(offset, 4) * 16, MOVE - WIN), 16)
        place = lax.broadcasted_iota(jnp.int32, (S, WIN), 0)
        inside = (place - landing) & (S - 1)
        source = lax.broadcasted_iota(jnp.int32, (S, WIN), 1)
        pick = jnp.where((source - (offset - start) == inside) & (inside < length), 1.0, 0.0).astype(BF)
        key_place = (lax.broadcasted_iota(jnp.int32, (S, GROUP * S), 0) - landing) & (S - 1)
        query_place = (lax.broadcasted_iota(jnp.int32, (S, GROUP * S), 1) - landing) & (S - 1)
        causal = key_place <= query_place
        allowed = causal & (query_place < length)
        window = pl.ds(start, WIN)
        all_k = dot(pick, k[window, :], NN).astype(BF)
        all_v = dot(pick, v[window, :], NN).astype(BF)
        if d >= 2:
            store(d - 2).wait()
        here = slot.at[d % 2]
        for n in range(nc):
            kd = all_k[:, HD * n : HD * (n + 1)]
            vd = all_v[:, HD * n : HD * (n + 1)]
            cols = slice(GROUP * HD * n, GROUP * HD * (n + 1))
            qs = heads_to_rows(dot(pick, q[window, cols], NN).astype(BF))
            gs = heads_to_rows(dot(pick, g[window, cols], NN).astype(BF))
            weights = transposed_softmax(dot(kd, qs, NT), allowed)
            logits = dot(vd, gs, NT)
            delta = jnp.sum(weights * logits, axis=0, keepdims=True)
            grad = (weights * (logits - delta)).astype(BF)
            weights = weights.astype(BF)
            dv = dot(weights, gs, NN).astype(BF)
            dk = (dot(grad, qs, NN) * SCALE).astype(BF)
            grad32 = grad.astype(F32)
            turned = jnp.concatenate([grad32[:, S * h : S * (h + 1)].T for h in range(GROUP)], axis=1)
            square = jnp.where(causal, weights.astype(F32), turned).astype(BF)
            base = KVROWS * n
            here[base : base + S, :] = square[:, :HD]
            here[base + S : base + 2 * S, :] = square[:, HD:]
            here[base + 2 * S : base + 3 * S, :] = kd
            here[base + 3 * S : base + 4 * S, :] = vd
            here[base + 4 * S : base + 5 * S, :] = dk
            here[base + 5 * S : base + 6 * S, :] = dv
        store(d).start()
    store(NDOC - 2).wait()
    store(NDOC - 1).wait()
    if with_meta:
        meta_copy.wait()


def send(table, q, k, v, g, kvs, with_meta):
    nc = len(kvs)
    height = KVROWS * nc + (META if with_meta else 0)
    any_spec = pl.BlockSpec(memory_space=pl.ANY)
    return pl.pallas_call(
        functools.partial(send_kernel, kvs, with_meta),
        out_shape=jax.ShapeDtypeStruct((NSLOT, height, HD), BF),
        in_specs=[pl.BlockSpec(memory_space=pltpu.SMEM)] + [any_spec] * 4,
        out_specs=any_spec,
        scratch_shapes=[
            pltpu.VMEM((MOVE, GROUP * HD * nc), BF),
            pltpu.VMEM((MOVE, HD * nc), BF),
            pltpu.VMEM((MOVE, HD * nc), BF),
            pltpu.VMEM((MOVE, GROUP * HD * nc), BF),
            pltpu.VMEM((2, KVROWS * nc, HD), BF),
            pltpu.VMEM((NSLOT, META, HD), BF),
            pltpu.SemaphoreType.DMA((4,)),
            pltpu.SemaphoreType.DMA((2,)),
            pltpu.SemaphoreType.DMA,
        ],
        compiler_params=pltpu.CompilerParams(vmem_limit_bytes=40 << 20),
        cost_estimate=pl.CostEstimate(flops=4_000_000_000 * nc // 4, bytes_accessed=10_000_000 * nc // 4, transcendentals=1_000_000),
        name="send",
    )(table, q, k, v, g)


def home_kernel(lengths, q, k, v, g, out, dq, dk, dv, acc_k, acc_v):
    block = 128
    ends = []
    total = jnp.int32(0)
    for i in range(6):
        total = total + lengths[0, i]
        ends.append(total)
    acc_k[...] = jnp.zeros_like(acc_k)
    acc_v[...] = jnp.zeros_like(acc_v)
    for b in range(3):
        low = max(0, block * (b - 1))
        span = block * (b + 1) - low
        rows = slice(block * b, block * (b + 1))
        keys = slice(low, low + span)
        position = block * b + (lax.broadcasted_iota(jnp.int32, (1, GROUP * block), 1) & (block - 1))
        start = jnp.zeros_like(position)
        for end in ends:
            start = jnp.where(position >= end, end, start)
        key_position = low + lax.broadcasted_iota(jnp.int32, (span, GROUP * block), 0)
        allowed = (key_position <= position) & (key_position >= start)
        qs, gs = heads_to_rows(q[rows, :]), heads_to_rows(g[rows, :])
        kb, vb = k[keys, :], v[keys, :]
        weights = transposed_softmax(dot(kb, qs, NT), allowed)
        logits = dot(vb, gs, NT)
        delta = jnp.sum(weights * logits, axis=0, keepdims=True)
        grad = (weights * (logits - delta)).astype(BF)
        weights = weights.astype(BF)
        acc_v[keys, :] += dot(weights, gs, NN)
        acc_k[keys, :] += dot(grad, qs, NN)
        turned_out = dot(vb, weights, TN)
        turned_dq = dot(kb, grad, TN) * SCALE
        for h in range(GROUP):
            lanes = slice(block * h, block * (h + 1))
            out[rows, HD * h : HD * (h + 1)] = turned_out[:, lanes].T.astype(BF)
            dq[rows, HD * h : HD * (h + 1)] = turned_dq[:, lanes].T.astype(BF)
    dk[...] = (acc_k[...] * SCALE).astype(BF)
    dv[...] = acc_v[...].astype(BF)


def home(lengths, q, k, v, g):
    total = q.shape[0]
    wide = pl.BlockSpec((HOME, GROUP * HD), lambda c: (0, c))
    narrow = pl.BlockSpec((HOME, HD), lambda c: (0, c))
    return pl.pallas_call(
        home_kernel,
        out_shape=[
            jax.ShapeDtypeStruct((total, KV * GROUP * HD), BF),
            jax.ShapeDtypeStruct((total, KV * GROUP * HD), BF),
            jax.ShapeDtypeStruct((total, KV * HD), BF),
            jax.ShapeDtypeStruct((total, KV * HD), BF),
        ],
        grid=(KV,),
        in_specs=[pl.BlockSpec(memory_space=pltpu.SMEM), wide, narrow, narrow, wide],
        out_specs=[wide, wide, narrow, narrow],
        scratch_shapes=[pltpu.VMEM((HOME, HD), F32), pltpu.VMEM((HOME, HD), F32)],
        compiler_params=pltpu.CompilerParams(vmem_limit_bytes=40 << 20),
        cost_estimate=pl.CostEstimate(flops=10_000_000_000, bytes_accessed=10_000_000, transcendentals=2_000_000),
        name="home",
    )(lengths, q, k, v, g)


def receive_kernel(kvs, sources, landings, recv, out_in, dq_in, dk_in, dv_in, out, dq, dk, dv, slot, o_buf, q_buf, k_buf, v_buf, in_sem, out_sem):
    nc = len(kvs)

    def load(d):
        return pltpu.make_async_copy(recv.at[sources[d], pl.ds(0, KVROWS * nc), :], slot.at[d], in_sem.at[d])

    for d in range(NDOC):
        load(d).start()
    o_buf[...] = jnp.zeros_like(o_buf)
    q_buf[...] = jnp.zeros_like(q_buf)
    k_buf[...] = jnp.zeros_like(k_buf)
    v_buf[...] = jnp.zeros_like(v_buf)
    wide_row = lax.broadcasted_iota(jnp.int32, (GROUP * S, GROUP * HD), 0) // S
    wide_col = lax.broadcasted_iota(jnp.int32, (GROUP * S, GROUP * HD), 1) // HD
    diagonal = wide_row == wide_col
    ones = jnp.where(diagonal, 1.0, 0.0).astype(BF)
    for d in range(NDOC):
        load(d).wait()
        landing = landings[d]
        shift = landing & (S - 1)
        first = pl.multiple_of(landing - shift, S)
        key_place = (lax.broadcasted_iota(jnp.int32, (S, GROUP * S), 0) - landing) & (S - 1)
        query_place = (lax.broadcasted_iota(jnp.int32, (S, GROUP * S), 1) - landing) & (S - 1)
        causal = key_place <= query_place

        def put(buf, cols, value):
            kept = lax.broadcasted_iota(jnp.int32, value.shape, 0) >= shift
            here, after = pl.ds(first, S), pl.ds(first + S, S)
            buf[here, cols] = jnp.where(kept, value, buf[here, cols].astype(F32)).astype(BF)
            buf[after, cols] = jnp.where(kept, buf[after, cols].astype(F32), value).astype(BF)

        for n in range(nc):
            base = KVROWS * n
            square = jnp.concatenate([slot[d, base : base + S, :], slot[d, base + S : base + 2 * S, :]], axis=1).astype(F32)
            weights = jnp.where(causal, square, 0.0).astype(BF)
            grad = jnp.where(causal, 0.0, square).astype(BF)
            kd = slot[d, base + 2 * S : base + 3 * S, :]
            vd = slot[d, base + 3 * S : base + 4 * S, :]
            attended = dot(weights, vd, TN)
            attended = jnp.concatenate([attended[S * h : S * (h + 1)] for h in range(GROUP)], axis=1)
            k4 = jnp.concatenate([kd.astype(F32)] * GROUP, axis=1)
            k16 = jnp.where(diagonal, jnp.concatenate([k4] * GROUP, axis=0), 0.0).astype(BF)
            query = (dot(grad, k16, NN) - dot(grad, ones, NN) * k4) * SCALE
            wide, narrow = slice(GROUP * HD * n, GROUP * HD * (n + 1)), slice(HD * n, HD * (n + 1))
            put(o_buf, wide, attended)
            put(q_buf, wide, query)
            put(k_buf, narrow, slot[d, base + 4 * S : base + 5 * S, :].astype(F32))
            put(v_buf, narrow, slot[d, base + 5 * S : base + 6 * S, :].astype(F32))
    rows, filled = pl.ds(HOME, MOVE), pl.ds(0, MOVE)
    wide, narrow = pl.ds(GROUP * HD * kvs[0], GROUP * HD * nc), pl.ds(HD * kvs[0], HD * nc)
    stores = [
        pltpu.make_async_copy(o_buf.at[filled, :], out.at[rows, wide], out_sem.at[0]),
        pltpu.make_async_copy(q_buf.at[filled, :], dq.at[rows, wide], out_sem.at[1]),
        pltpu.make_async_copy(k_buf.at[filled, :], dk.at[rows, narrow], out_sem.at[2]),
        pltpu.make_async_copy(v_buf.at[filled, :], dv.at[rows, narrow], out_sem.at[3]),
    ]
    for copy in stores:
        copy.start()
    for copy in stores:
        copy.wait()


def receive(sources, landings, recv, outs, kvs):
    nc = len(kvs)
    any_spec = pl.BlockSpec(memory_space=pl.ANY)
    smem = pl.BlockSpec(memory_space=pltpu.SMEM)
    padded = MOVE + S
    return pl.pallas_call(
        functools.partial(receive_kernel, kvs),
        out_shape=[jax.ShapeDtypeStruct(o.shape, o.dtype) for o in outs],
        in_specs=[smem, smem] + [any_spec] * 5,
        out_specs=[any_spec] * 4,
        input_output_aliases={3: 0, 4: 1, 5: 2, 6: 3},
        scratch_shapes=[
            pltpu.VMEM((NDOC, KVROWS * nc, HD), BF),
            pltpu.VMEM((padded, GROUP * HD * nc), BF),
            pltpu.VMEM((padded, GROUP * HD * nc), BF),
            pltpu.VMEM((padded, HD * nc), BF),
            pltpu.VMEM((padded, HD * nc), BF),
            pltpu.SemaphoreType.DMA((NDOC,)),
            pltpu.SemaphoreType.DMA((4,)),
        ],
        compiler_params=pltpu.CompilerParams(vmem_limit_bytes=40 << 20),
        cost_estimate=pl.CostEstimate(flops=4_000_000_000 * nc // 4, bytes_accessed=10_000_000 * nc // 4, transcendentals=0),
        name="receive",
    )(sources, landings, recv, *outs)


def placement(codes):
    valid = codes > 0
    rank = jnp.sum((valid[None, :] & (codes[None, :] < codes[:, None])).astype(jnp.int32), axis=1)
    order = jnp.arange(NDOC, dtype=jnp.int32)
    chosen = (valid[None, :] & (rank[None, :] == order[:, None])).astype(jnp.int32)
    sources = jnp.sum(chosen * jnp.arange(NSLOT, dtype=jnp.int32)[None, :], axis=1)
    landings = jnp.sum(chosen * (codes - 1)[None, :], axis=1)
    return sources, landings


def codes_of(meta):
    pairs = meta.astype(F32).astype(jnp.int32)
    return pairs[:, 0] * 32 + pairs[:, S]


def swap(x, axis, size, mask):
    return lax.ppermute(x, axis, [(i, i ^ mask) for i in range(size)])


def add(*terms):
    total = terms[0].astype(F32)
    for term in terms[1:]:
        total = total + term.astype(F32)
    return total


def reduce_x(layer_grad):
    columns = layer_grad.shape[-1]
    grad = layer_grad.reshape(2, 4, 2, 256, columns)
    core, x = lax.axis_index("core"), lax.axis_index("x")
    mine = lax.dynamic_index_in_dim(grad, core, 2, keepdims=False)
    other = lax.dynamic_index_in_dim(grad, 1 - core, 2, keepdims=False)
    part = add(mine, swap(other, "core", 2, 1)).astype(BF)

    def block(step):
        return lax.dynamic_index_in_dim(part, (x + step) % 4, 1, keepdims=False)

    received = [lax.ppermute(block(step), "x", [(i, (i + step) % 4) for i in range(4)]) for step in (1, 2, 3)]
    return add(block(0), *received).astype(BF)


def reduce_rest(part):
    yhi = lax.axis_index("yhi")
    mine = lax.dynamic_index_in_dim(part, yhi, 0, keepdims=False)
    other = lax.dynamic_index_in_dim(part, 1 - yhi, 0, keepdims=False)
    total = add(mine, swap(other, "yhi", 2, 1))
    for axis, size, mask in (("ylo", 2, 1), ("z", 4, 1), ("z", 4, 2)):
        total = total.astype(BF)
        total = add(total, swap(total, axis, size, mask))
    total = total.astype(BF)
    twin = swap(total, "core", 2, 1)
    core = lax.axis_index("core")
    first = jnp.where(core == 0, total, twin)
    second = jnp.where(core == 0, twin, total)
    return jnp.concatenate([first, second], axis=0).astype(F32)


def exchange(slots):
    return lax.all_to_all(slots, DP, split_axis=0, concat_axis=0, tiled=True)


def per_device(q, k, v, g, home_lengths, moved_lengths, moved_offsets, moved_owner, owner_offsets, layer_grad):
    table = jnp.concatenate([moved_lengths, moved_offsets, moved_owner, owner_offsets], axis=0)
    everything = tuple(range(KV))
    part = reduce_x(layer_grad)
    received = exchange(send(table, q, k, v, g, everything, True))
    outs = home(home_lengths, q, k, v, g)
    sources, landings = placement(codes_of(received[:, KVROWS * KV, :]))
    outs = receive(sources, landings, received, outs, everything)
    part, received = lax.optimization_barrier((part, received))
    return (*outs, reduce_rest(part))


def solution(mesh):
    fine = Mesh(mesh.devices.reshape(2, 4, 2, 2, 4), FINE)
    rows = P(FINE, None)
    return jax.shard_map(
        per_device,
        mesh=fine,
        in_specs=(rows,) * 9 + (P(DP, ("yhi", "x"), None, None),),
        out_specs=(rows, rows, rows, rows, P(("yhi", "x"), None)),
        check_vma=False,
    )
```

```python
import functools
import math

import jax
import jax.numpy as jnp
from jax import lax
from jax.experimental import pallas as pl
from jax.experimental.pallas import tpu as pltpu
from jax.sharding import Mesh
from jax.sharding import PartitionSpec as P

HD = 128
HOME = 384
S = 64
MOVE = 512
NDOC = 8
GROUP = 4
KV = 4
WIN = 80
NSLOT = 16
KVROWS = 6 * S
META = 8
SCALE = 1.0 / math.sqrt(HD)
EXP2_SCALE = SCALE * math.log2(math.e)
FINE = ("ylo", "z", "core", "yhi", "x")
DP = ("ylo", "z", "core")
BF = jnp.bfloat16
F32 = jnp.float32


def dot(a, b, dims):
    return lax.dot_general(a, b, (dims, ((), ())), preferred_element_type=F32)


NN = ((1,), (0,))
NT = ((1,), (1,))
TN = ((0,), (0,))


def heads_to_rows(x):
    return jnp.concatenate([x[:, HD * h : HD * (h + 1)] for h in range(GROUP)], axis=0)


def transposed_softmax(scores, allowed, filled=None):
    scores = jnp.where(allowed, scores * EXP2_SCALE, -1e30)
    highest = jnp.max(scores, axis=0, keepdims=True)
    exponent = jnp.exp2(scores - highest)
    inverse = 1.0 / jnp.sum(exponent, axis=0, keepdims=True)
    if filled is not None:
        inverse = jnp.where(filled, inverse, 0.0)
    return exponent * inverse


def send_kernel(table, q_hbm, k_hbm, v_hbm, g_hbm, *refs):
    out, q, k, v, g, slot, meta, in_sem, out_sem, meta_sem = refs
    chunk = 128
    pairs = ((q_hbm, q), (g_hbm, g), (k_hbm, k), (v_hbm, v))

    def load(a, b):
        source, target = pairs[a]
        return pltpu.make_async_copy(source.at[pl.ds(HOME + chunk * b, chunk), :], target.at[pl.ds(chunk * b, chunk), :], in_sem.at[a, b])

    for b in range(MOVE // chunk):
        for a in range(4):
            load(a, b).start()
    lane = lax.broadcasted_iota(jnp.int32, (META, HD), 1)
    for s in range(NSLOT):
        code = jnp.int32(0)
        for d in range(NDOC):
            code = code + jnp.where(table[2, d] == s, table[3, d] + 1, 0)
        meta[s] = jnp.where(lane < S, lax.shift_right_logical(code, 5), code & 31).astype(F32).astype(BF)

    meta_copy = pltpu.make_async_copy(meta, out.at[:, pl.ds(KVROWS * KV, META), :], meta_sem)
    meta_copy.start()

    def store(d):
        return pltpu.make_async_copy(slot.at[d % 2], out.at[table[2, d], pl.ds(0, KVROWS * KV), :], out_sem.at[d % 2])

    same = (lax.broadcasted_iota(jnp.int32, (HD, HD), 0) & (S - 1)) == (lax.broadcasted_iota(jnp.int32, (HD, HD), 1) & (S - 1))
    loaded = -1
    for d in range(NDOC):
        last = min((S * d + WIN - 1) // chunk, MOVE // chunk - 1)
        while loaded < last:
            loaded += 1
            for a in range(4):
                load(a, loaded).wait()
        length, offset, landing = table[0, d], table[1, d], table[3, d]
        start = pl.multiple_of(jnp.minimum(lax.shift_right_logical(offset, 4) * 16, MOVE - WIN), 16)
        inside = (lax.broadcasted_iota(jnp.int32, (S, WIN), 0) - landing) & (S - 1)
        source = lax.broadcasted_iota(jnp.int32, (S, WIN), 1)
        pick = jnp.where((source - (offset - start) == inside) & (inside < length), 1.0, 0.0).astype(BF)
        key_place = (lax.broadcasted_iota(jnp.int32, (S, 1), 0) - landing) & (S - 1)
        query_place = (lax.broadcasted_iota(jnp.int32, (1, GROUP * S), 1) - landing) & (S - 1)
        filled = query_place < length
        allowed = key_place <= jnp.where(filled, query_place, -1)
        window = pl.ds(start, WIN)
        all_k = dot(pick, k[window, :], NN).astype(BF)
        all_v = dot(pick, v[window, :], NN).astype(BF)
        if d >= 2:
            store(d - 2).wait()
        here = slot.at[d % 2]
        for n in range(KV):
            kd = all_k[:, HD * n : HD * (n + 1)]
            vd = all_v[:, HD * n : HD * (n + 1)]
            cols = slice(GROUP * HD * n, GROUP * HD * (n + 1))
            qs = heads_to_rows(dot(pick, q[window, cols], NN).astype(BF))
            gs = heads_to_rows(dot(pick, g[window, cols], NN).astype(BF))
            weights = transposed_softmax(dot(kd, qs, NT), allowed, filled)
            logits = dot(vd, gs, NT)
            delta = jnp.sum(weights * logits, axis=0, keepdims=True)
            grad = weights * (logits - delta)
            dv = dot(weights.astype(BF), gs, NN).astype(BF)
            dk = (dot(grad.astype(BF), qs, NN) * SCALE).astype(BF)
            turned = jnp.concatenate([grad[:, :HD], grad[:, HD:]], axis=0).T
            square = jnp.concatenate([weights[:, :HD], weights[:, HD:]], axis=0) + jnp.where(same, 0.0, turned)
            base = KVROWS * n
            here[base : base + 2 * S, :] = square.astype(BF)
            here[base + 2 * S : base + 3 * S, :] = kd
            here[base + 3 * S : base + 4 * S, :] = vd
            here[base + 4 * S : base + 5 * S, :] = dk
            here[base + 5 * S : base + 6 * S, :] = dv
        store(d).start()
    store(NDOC - 2).wait()
    store(NDOC - 1).wait()
    meta_copy.wait()


def send(table, q, k, v, g):
    hbm = pl.BlockSpec(memory_space=pltpu.HBM)
    return pl.pallas_call(
        send_kernel,
        out_shape=jax.ShapeDtypeStruct((NSLOT, KVROWS * KV + META, HD), BF),
        in_specs=[pl.BlockSpec(memory_space=pltpu.SMEM)] + [hbm] * 4,
        out_specs=hbm,
        scratch_shapes=[
            pltpu.VMEM((MOVE, KV * GROUP * HD), BF),
            pltpu.VMEM((MOVE, KV * HD), BF),
            pltpu.VMEM((MOVE, KV * HD), BF),
            pltpu.VMEM((MOVE, KV * GROUP * HD), BF),
            pltpu.VMEM((2, KVROWS * KV, HD), BF),
            pltpu.VMEM((NSLOT, META, HD), BF),
            pltpu.SemaphoreType.DMA((4, 4)),
            pltpu.SemaphoreType.DMA((2,)),
            pltpu.SemaphoreType.DMA,
        ],
        cost_estimate=pl.CostEstimate(flops=4_000_000_000, bytes_accessed=10_000_000, transcendentals=1_000_000),
        name="send",
    )(table, q, k, v, g)


def home_kernel(lengths, q, k, v, g, out, dq, dk, dv, acc_k, acc_v):
    block = 128
    ends = []
    total = jnp.int32(0)
    for i in range(6):
        total = total + lengths[0, i]
        ends.append(total)
    acc_k[...] = jnp.zeros_like(acc_k)
    acc_v[...] = jnp.zeros_like(acc_v)
    for b in range(3):
        low = max(0, block * (b - 1))
        span = block * (b + 1) - low
        rows = slice(block * b, block * (b + 1))
        keys = slice(low, low + span)
        position = block * b + (lax.broadcasted_iota(jnp.int32, (1, GROUP * block), 1) & (block - 1))
        start = jnp.zeros_like(position)
        for end in ends:
            start = jnp.where(position >= end, end, start)
        key_position = low + lax.broadcasted_iota(jnp.int32, (span, GROUP * block), 0)
        allowed = (key_position <= position) & (key_position >= start)
        qs, gs = heads_to_rows(q[rows, :]), heads_to_rows(g[rows, :])
        kb, vb = k[keys, :], v[keys, :]
        weights = transposed_softmax(dot(kb, qs, NT), allowed)
        logits = dot(vb, gs, NT)
        delta = jnp.sum(weights * logits, axis=0, keepdims=True)
        grad = (weights * (logits - delta)).astype(BF)
        weights = weights.astype(BF)
        acc_v[keys, :] += dot(weights, gs, NN)
        acc_k[keys, :] += dot(grad, qs, NN)
        turned_out = dot(vb, weights, TN)
        turned_dq = dot(kb, grad, TN) * SCALE
        for h in range(GROUP):
            lanes = slice(block * h, block * (h + 1))
            out[rows, HD * h : HD * (h + 1)] = turned_out[:, lanes].T.astype(BF)
            dq[rows, HD * h : HD * (h + 1)] = turned_dq[:, lanes].T.astype(BF)
    dk[...] = (acc_k[...] * SCALE).astype(BF)
    dv[...] = acc_v[...].astype(BF)


def home(lengths, q, k, v, g):
    total = q.shape[0]
    wide = pl.BlockSpec((HOME, GROUP * HD), lambda c: (0, c))
    narrow = pl.BlockSpec((HOME, HD), lambda c: (0, c))
    return pl.pallas_call(
        home_kernel,
        out_shape=[
            jax.ShapeDtypeStruct((total, KV * GROUP * HD), BF),
            jax.ShapeDtypeStruct((total, KV * GROUP * HD), BF),
            jax.ShapeDtypeStruct((total, KV * HD), BF),
            jax.ShapeDtypeStruct((total, KV * HD), BF),
        ],
        grid=(KV,),
        in_specs=[pl.BlockSpec(memory_space=pltpu.SMEM), wide, narrow, narrow, wide],
        out_specs=[wide, wide, narrow, narrow],
        scratch_shapes=[pltpu.VMEM((HOME, HD), F32), pltpu.VMEM((HOME, HD), F32)],
        cost_estimate=pl.CostEstimate(flops=10_000_000_000, bytes_accessed=10_000_000, transcendentals=2_000_000),
        name="home",
    )(lengths, q, k, v, g)


def receive_kernel(sources, landings, recv, *refs):
    out, dq, dk, dv = refs[4:8]
    slot, o_buf, q_buf, k_buf, v_buf, o_out, q_out, k_out, v_out, in_sem, out_sem = refs[8:]

    def load(d, n):
        rows = pl.ds(KVROWS * n, KVROWS)
        return pltpu.make_async_copy(recv.at[sources[d], rows, :], slot.at[d, rows, :], in_sem.at[d, n])

    for n in range(KV):
        for d in range(NDOC):
            load(d, n).start()

    def stores(n):
        rows, wide, narrow = pl.ds(HOME, MOVE), pl.ds(GROUP * HD * n, GROUP * HD), pl.ds(HD * n, HD)
        return [
            pltpu.make_async_copy(o_out.at[n % 2], out.at[rows, wide], out_sem.at[0, n % 2]),
            pltpu.make_async_copy(q_out.at[n % 2], dq.at[rows, wide], out_sem.at[1, n % 2]),
            pltpu.make_async_copy(k_out.at[n % 2], dk.at[rows, narrow], out_sem.at[2, n % 2]),
            pltpu.make_async_copy(v_out.at[n % 2], dv.at[rows, narrow], out_sem.at[3, n % 2]),
        ]

    zeros = jnp.zeros((S, HD), BF)
    one = jnp.ones((S, HD), BF)
    ones = jnp.concatenate([jnp.concatenate([one, zeros], axis=1), jnp.concatenate([zeros, one], axis=1)], axis=0)

    def twice(x):
        return jnp.concatenate([jnp.concatenate([x, zeros], axis=1), jnp.concatenate([zeros, x], axis=1)], axis=0)

    def spread_heads(x):
        return jnp.concatenate([x[:S, :HD], x[S:, :HD], x[:S, HD:], x[S:, HD:]], axis=1)

    row = lax.broadcasted_iota(jnp.int32, (HD, 1), 0)
    column = lax.broadcasted_iota(jnp.int32, (1, HD), 1)
    shared = 6 * S
    for buf in (o_buf, q_buf, k_buf, v_buf):
        buf[shared:, :] = jnp.zeros((MOVE + S - shared, buf.shape[1]), F32)
    for n in range(KV):
        for d in range(NDOC):
            load(d, n).wait()
            landing = landings[d]
            shift = landing & (S - 1)
            first = pl.multiple_of(landing - shift, S)
            causal = ((row - landing) & (S - 1)) <= ((column - landing) & (S - 1))
            base = KVROWS * n
            square = slot[d, base : base + 2 * S, :].astype(F32)
            weights = jnp.where(causal, square, 0.0)
            grad = (square - weights).astype(BF)
            kd = slot[d, base + 2 * S : base + 3 * S, :]
            vd = slot[d, base + 3 * S : base + 4 * S, :]
            attended = dot(weights.T.astype(BF), twice(vd), NN)
            k32 = kd.astype(F32)
            k22 = jnp.concatenate([jnp.concatenate([k32, k32], axis=1)] * 2, axis=0)
            query = (dot(grad, twice(kd), NN) - dot(grad, ones, NN) * k22) * SCALE

            def put(buf, value):
                kept = lax.broadcasted_iota(jnp.int32, value.shape, 0) >= shift
                pltpu.store(buf.at[pl.ds(first, S), :], value, mask=kept)
                pltpu.store(buf.at[pl.ds(first + S, S), :], value, mask=jnp.logical_not(kept))

            put(o_buf, spread_heads(attended))
            put(q_buf, spread_heads(query))
            put(k_buf, slot[d, base + 4 * S : base + 5 * S, :].astype(F32))
            put(v_buf, slot[d, base + 5 * S : base + 6 * S, :].astype(F32))
        if n >= 2:
            for copy in stores(n - 2):
                copy.wait()
        for buf, final in ((o_buf, o_out), (q_buf, q_out), (k_buf, k_out), (v_buf, v_out)):
            final[n % 2] = buf[:MOVE, :].astype(BF)
        for copy in stores(n):
            copy.start()
    for n in (KV - 2, KV - 1):
        for copy in stores(n):
            copy.wait()


def receive(sources, landings, recv, outs):
    hbm = pl.BlockSpec(memory_space=pltpu.HBM)
    smem = pl.BlockSpec(memory_space=pltpu.SMEM)
    padded = MOVE + S
    wide, narrow = GROUP * HD, HD
    return pl.pallas_call(
        receive_kernel,
        out_shape=[jax.ShapeDtypeStruct(o.shape, o.dtype) for o in outs],
        in_specs=[smem, smem] + [hbm] * 5,
        out_specs=[hbm] * 4,
        input_output_aliases={3 + i: i for i in range(4)},
        scratch_shapes=[
            pltpu.VMEM((NDOC, KVROWS * KV, HD), BF),
            pltpu.VMEM((padded, wide), F32),
            pltpu.VMEM((padded, wide), F32),
            pltpu.VMEM((padded, narrow), F32),
            pltpu.VMEM((padded, narrow), F32),
            pltpu.VMEM((2, MOVE, wide), BF),
            pltpu.VMEM((2, MOVE, wide), BF),
            pltpu.VMEM((2, MOVE, narrow), BF),
            pltpu.VMEM((2, MOVE, narrow), BF),
            pltpu.SemaphoreType.DMA((NDOC, KV)),
            pltpu.SemaphoreType.DMA((4, 2)),
        ],
        cost_estimate=pl.CostEstimate(flops=4_000_000_000, bytes_accessed=10_000_000, transcendentals=0),
        name="receive",
    )(sources, landings, recv, *outs)


def placement(codes):
    valid = codes > 0
    rank = jnp.sum((valid[None, :] & (codes[None, :] < codes[:, None])).astype(jnp.int32), axis=1)
    order = jnp.arange(NDOC, dtype=jnp.int32)
    chosen = valid[None, :] & (rank[None, :] == order[:, None])
    sources = jnp.sum(jnp.where(chosen, jnp.arange(NSLOT, dtype=jnp.int32)[None, :], 0), axis=1)
    landings = jnp.sum(jnp.where(chosen, (codes - 1)[None, :], 0), axis=1)
    return sources, landings


def codes_of(meta):
    pairs = meta.astype(F32).astype(jnp.int32)
    return pairs[:, 0] * 32 + pairs[:, S]


def swap(x, axis, size, mask):
    return lax.ppermute(x, axis, [(i, i ^ mask) for i in range(size)])


def add(*terms):
    total = terms[0].astype(F32)
    for term in terms[1:]:
        total = total + term.astype(F32)
    return total


def shifts(pieces, axis, size):
    return [lax.ppermute(pieces(step), axis, [(i, (i + step) % size) for i in range(size)]) for step in range(1, size)]


def reduce_cores(layer_grad):
    grad = layer_grad.reshape(2, 4, 2, 4, 64, layer_grad.shape[-1])
    core = lax.axis_index("core")
    mine = lax.dynamic_index_in_dim(grad, core, 2, keepdims=False)
    other = lax.dynamic_index_in_dim(grad, 1 - core, 2, keepdims=False)
    return add(mine, swap(other, "core", 2, 1)).astype(BF)


def reduce_ring(part, axis, dim):
    place = lax.axis_index(axis)

    def block(step):
        return lax.dynamic_index_in_dim(part, (place + step) % 4, dim, keepdims=False)

    return add(block(0), *shifts(block, axis, 4)).astype(BF)


def spread(total):
    place = lax.axis_index("z")
    held = jnp.stack([total] + shifts(lambda step: total, "z", 4))
    half = jnp.concatenate([lax.dynamic_index_in_dim(held, (place - b) % 4, 0, keepdims=False) for b in range(4)], axis=0)
    twin = swap(half, "core", 2, 1)
    core = lax.axis_index("core")
    first = jnp.where(core == 0, half, twin)
    second = jnp.where(core == 0, twin, half)
    return jnp.concatenate([first, second], axis=0).astype(F32)


def exchange(slots):
    return lax.all_to_all(slots, DP, split_axis=0, concat_axis=0, tiled=True)


def per_device(q, k, v, g, home_lengths, moved_lengths, moved_offsets, moved_owner, owner_offsets, layer_grad):
    table = jnp.concatenate([moved_lengths, moved_offsets, moved_owner, owner_offsets], axis=0)
    received = exchange(send(table, q, k, v, g))
    part = reduce_cores(layer_grad)
    part = reduce_ring(part, "x", 1)
    outs = home(home_lengths, q, k, v, g)
    part, outs = lax.optimization_barrier((part, outs))
    part = reduce_ring(part, "z", 1)
    part, received = lax.optimization_barrier((part, received))
    yhi = lax.axis_index("yhi")
    mine = lax.dynamic_index_in_dim(part, yhi, 0, keepdims=False)
    theirs = swap(lax.dynamic_index_in_dim(part, 1 - yhi, 0, keepdims=False), "yhi", 2, 1)
    sources, landings = placement(codes_of(received[:, KVROWS * KV, :]))
    outs = receive(sources, landings, received, outs)
    theirs, outs = lax.optimization_barrier((theirs, outs))
    total = add(mine, theirs).astype(BF)
    total = add(total, swap(total, "ylo", 2, 1)).astype(BF)
    return (*outs, spread(total))


def solution(mesh):
    fine = Mesh(mesh.devices.reshape(2, 4, 2, 2, 4), FINE)
    rows = P(FINE, None)
    return jax.shard_map(
        per_device,
        mesh=fine,
        in_specs=(rows,) * 9 + (P(DP, ("yhi", "x"), None, None),),
        out_specs=(rows, rows, rows, rows, P(("yhi", "x"), None)),
        check_vma=False,
    )
```

```python
import functools
import math

import jax
import jax.numpy as jnp
from jax import lax
from jax.experimental import pallas as pl
from jax.experimental.pallas import tpu as pltpu
from jax.sharding import Mesh
from jax.sharding import PartitionSpec as P

HD = 128
HOME = 384
S = 64
MOVE = 512
NDOC = 8
GROUP = 4
KV = 4
WIN = 80
NSLOT = 16
NFAR = 8
KVROWS = 6 * S
META = 8
SCALE = 1.0 / math.sqrt(HD)
EXP2_SCALE = SCALE * math.log2(math.e)
FINE = ("ylo", "z", "core", "yhi", "x")
DP = ("ylo", "z", "core")
BF = jnp.bfloat16
F32 = jnp.float32


def dot(a, b, dims):
    return lax.dot_general(a, b, (dims, ((), ())), preferred_element_type=F32)


NN = ((1,), (0,))
NT = ((1,), (1,))
TN = ((0,), (0,))


def heads_to_rows(x):
    return jnp.concatenate([x[:, HD * h : HD * (h + 1)] for h in range(GROUP)], axis=0)


def transposed_softmax(scores, allowed, filled=None):
    scores = jnp.where(allowed, scores * EXP2_SCALE, -1e30)
    highest = jnp.max(scores, axis=0, keepdims=True)
    exponent = jnp.exp2(scores - highest)
    inverse = 1.0 / jnp.sum(exponent, axis=0, keepdims=True)
    if filled is not None:
        inverse = jnp.where(filled, inverse, 0.0)
    return exponent * inverse


def send_kernel(table, q_hbm, k_hbm, v_hbm, g_hbm, *refs):
    near, far = refs[0], refs[1 : 1 + NFAR]
    q, k, v, g, slot, meta, in_sem, out_sem, meta_sem = refs[1 + NFAR :]
    chunk = 128
    pairs = ((q_hbm, q), (g_hbm, g), (k_hbm, k), (v_hbm, v))

    def load(a, b):
        source, target = pairs[a]
        return pltpu.make_async_copy(source.at[pl.ds(HOME + chunk * b, chunk), :], target.at[pl.ds(chunk * b, chunk), :], in_sem.at[a, b])

    for b in range(MOVE // chunk):
        for a in range(4):
            load(a, b).start()
    lane = lax.broadcasted_iota(jnp.int32, (META, HD), 1)
    for s in range(NSLOT):
        code = jnp.int32(0)
        for d in range(NDOC):
            code = code + jnp.where(table[2, d] == s, table[3, d] + 1, 0)
        meta[s] = jnp.where(lane < S, lax.shift_right_logical(code, 5), code & 31).astype(F32).astype(BF)

    body, tail = pl.ds(0, KVROWS * KV), pl.ds(KVROWS * KV, META)
    meta_copies = [pltpu.make_async_copy(meta.at[pl.ds(0, NFAR)], near.at[:, tail, :], meta_sem.at[NFAR])]
    meta_copies += [pltpu.make_async_copy(meta.at[NFAR + m], far[m].at[tail, :], meta_sem.at[m]) for m in range(NFAR)]
    for copy in meta_copies:
        copy.start()

    def store_near(d):
        return pltpu.make_async_copy(slot.at[d % 2], near.at[table[2, d] & (NFAR - 1), body, :], out_sem.at[d % 2])

    def store_far(d, m):
        return pltpu.make_async_copy(slot.at[d % 2], far[m].at[body, :], out_sem.at[d % 2])

    def store(d):
        @pl.when(table[2, d] < NFAR)
        def _():
            store_near(d).start()

        for m in range(NFAR):

            @pl.when(table[2, d] == NFAR + m)
            def _(m=m):
                store_far(d, m).start()

    same = (lax.broadcasted_iota(jnp.int32, (HD, HD), 0) & (S - 1)) == (lax.broadcasted_iota(jnp.int32, (HD, HD), 1) & (S - 1))
    loaded = -1
    for d in range(NDOC):
        last = min((S * d + WIN - 1) // chunk, MOVE // chunk - 1)
        while loaded < last:
            loaded += 1
            for a in range(4):
                load(a, loaded).wait()
        length, offset, landing = table[0, d], table[1, d], table[3, d]
        start = pl.multiple_of(jnp.minimum(lax.shift_right_logical(offset, 4) * 16, MOVE - WIN), 16)
        inside = (lax.broadcasted_iota(jnp.int32, (S, WIN), 0) - landing) & (S - 1)
        source = lax.broadcasted_iota(jnp.int32, (S, WIN), 1)
        pick = jnp.where((source - (offset - start) == inside) & (inside < length), 1.0, 0.0).astype(BF)
        key_place = (lax.broadcasted_iota(jnp.int32, (S, 1), 0) - landing) & (S - 1)
        query_place = (lax.broadcasted_iota(jnp.int32, (1, GROUP * S), 1) - landing) & (S - 1)
        filled = query_place < length
        allowed = key_place <= jnp.where(filled, query_place, -1)
        window = pl.ds(start, WIN)
        all_k = dot(pick, k[window, :], NN).astype(BF)
        all_v = dot(pick, v[window, :], NN).astype(BF)
        if d >= 2:
            store_far(d - 2, 0).wait()
        here = slot.at[d % 2]
        each = range(KV)
        wide = [slice(GROUP * HD * n, GROUP * HD * (n + 1)) for n in each]
        kd = [all_k[:, HD * n : HD * (n + 1)] for n in each]
        vd = [all_v[:, HD * n : HD * (n + 1)] for n in each]
        qs = [heads_to_rows(dot(pick, q[window, wide[n]], NN).astype(BF)) for n in each]
        gs = [heads_to_rows(dot(pick, g[window, wide[n]], NN).astype(BF)) for n in each]
        scores = [dot(kd[n], qs[n], NT) for n in each]
        logits = [dot(vd[n], gs[n], NT) for n in each]
        weights = [transposed_softmax(scores[n], allowed, filled) for n in each]
        delta = [jnp.sum(weights[n] * logits[n], axis=0, keepdims=True) for n in each]
        grad = [weights[n] * (logits[n] - delta[n]) for n in each]
        both = [jnp.concatenate([weights[n].astype(BF), grad[n].astype(BF)], axis=0) for n in each]
        summed = [dot(both[n], jnp.concatenate([gs[n], qs[n]], axis=1), NN) for n in each]
        for n in each:
            turned = jnp.concatenate([grad[n][:, :HD], grad[n][:, HD:]], axis=0).T
            square = jnp.concatenate([weights[n][:, :HD], weights[n][:, HD:]], axis=0) + jnp.where(same, 0.0, turned)
            base = KVROWS * n
            here[base : base + 2 * S, :] = square.astype(BF)
            here[base + 2 * S : base + 3 * S, :] = kd[n]
            here[base + 3 * S : base + 4 * S, :] = vd[n]
            here[base + 4 * S : base + 5 * S, :] = (summed[n][S:, HD:] * SCALE).astype(BF)
            here[base + 5 * S : base + 6 * S, :] = summed[n][:S, :HD].astype(BF)
        store(d)
    store_far(NDOC - 2, 0).wait()
    store_far(NDOC - 1, 0).wait()
    for copy in meta_copies:
        copy.wait()


def send(table, q, k, v, g):
    hbm = pl.BlockSpec(memory_space=pltpu.HBM)
    return pl.pallas_call(
        send_kernel,
        out_shape=[jax.ShapeDtypeStruct((NFAR, KVROWS * KV + META, HD), BF)] + [jax.ShapeDtypeStruct((KVROWS * KV + META, HD), BF)] * NFAR,
        in_specs=[pl.BlockSpec(memory_space=pltpu.SMEM)] + [hbm] * 4,
        out_specs=[hbm] * (1 + NFAR),
        scratch_shapes=[
            pltpu.VMEM((MOVE, KV * GROUP * HD), BF),
            pltpu.VMEM((MOVE, KV * HD), BF),
            pltpu.VMEM((MOVE, KV * HD), BF),
            pltpu.VMEM((MOVE, KV * GROUP * HD), BF),
            pltpu.VMEM((2, KVROWS * KV, HD), BF),
            pltpu.VMEM((NSLOT, META, HD), BF),
            pltpu.SemaphoreType.DMA((4, 4)),
            pltpu.SemaphoreType.DMA((2,)),
            pltpu.SemaphoreType.DMA((1 + NFAR,)),
        ],
        cost_estimate=pl.CostEstimate(flops=4_000_000_000, bytes_accessed=10_000_000, transcendentals=1_000_000),
        name="send",
    )(table, q, k, v, g)


def home_kernel(lengths, q, k, v, g, out, dq, dk, dv, acc_k, acc_v):
    block = 128
    ends = []
    total = jnp.int32(0)
    for i in range(6):
        total = total + lengths[0, i]
        ends.append(total)
    acc_k[...] = jnp.zeros_like(acc_k)
    acc_v[...] = jnp.zeros_like(acc_v)
    for b in range(3):
        low = max(0, block * (b - 1))
        span = block * (b + 1) - low
        rows = slice(block * b, block * (b + 1))
        keys = slice(low, low + span)
        position = block * b + (lax.broadcasted_iota(jnp.int32, (1, GROUP * block), 1) & (block - 1))
        start = jnp.zeros_like(position)
        for end in ends:
            start = jnp.where(position >= end, end, start)
        key_position = low + lax.broadcasted_iota(jnp.int32, (span, GROUP * block), 0)
        allowed = (key_position <= position) & (key_position >= start)
        qs, gs = heads_to_rows(q[rows, :]), heads_to_rows(g[rows, :])
        kb, vb = k[keys, :], v[keys, :]
        weights = transposed_softmax(dot(kb, qs, NT), allowed)
        logits = dot(vb, gs, NT)
        delta = jnp.sum(weights * logits, axis=0, keepdims=True)
        grad = (weights * (logits - delta)).astype(BF)
        weights = weights.astype(BF)
        acc_v[keys, :] += dot(weights, gs, NN)
        acc_k[keys, :] += dot(grad, qs, NN)
        turned_out = dot(vb, weights, TN)
        turned_dq = dot(kb, grad, TN) * SCALE
        for h in range(GROUP):
            lanes = slice(block * h, block * (h + 1))
            out[rows, HD * h : HD * (h + 1)] = turned_out[:, lanes].T.astype(BF)
            dq[rows, HD * h : HD * (h + 1)] = turned_dq[:, lanes].T.astype(BF)
    dk[...] = (acc_k[...] * SCALE).astype(BF)
    dv[...] = acc_v[...].astype(BF)


def home(lengths, q, k, v, g):
    total = q.shape[0]
    wide = pl.BlockSpec((HOME, GROUP * HD), lambda c: (0, c))
    narrow = pl.BlockSpec((HOME, HD), lambda c: (0, c))
    return pl.pallas_call(
        home_kernel,
        out_shape=[
            jax.ShapeDtypeStruct((total, KV * GROUP * HD), BF),
            jax.ShapeDtypeStruct((total, KV * GROUP * HD), BF),
            jax.ShapeDtypeStruct((total, KV * HD), BF),
            jax.ShapeDtypeStruct((total, KV * HD), BF),
        ],
        grid=(KV,),
        in_specs=[pl.BlockSpec(memory_space=pltpu.SMEM), wide, narrow, narrow, wide],
        out_specs=[wide, wide, narrow, narrow],
        scratch_shapes=[pltpu.VMEM((HOME, HD), F32), pltpu.VMEM((HOME, HD), F32)],
        cost_estimate=pl.CostEstimate(flops=10_000_000_000, bytes_accessed=10_000_000, transcendentals=2_000_000),
        name="home",
    )(lengths, q, k, v, g)


def receive_kernel(sources, landings, near, *refs):
    far = refs[:NFAR]
    out, dq, dk, dv = refs[NFAR + 4 : NFAR + 8]
    slot, o_buf, q_buf, k_buf, v_buf, o_out, q_out, k_out, v_out, in_sem, out_sem = refs[NFAR + 8 :]

    def load(d, n, m=0):
        rows = pl.ds(KVROWS * n, KVROWS)
        return pltpu.make_async_copy(far[m].at[rows, :], slot.at[d, rows, :], in_sem.at[d, n])

    for d in range(NDOC):

        @pl.when(sources[d] < NFAR)
        def _(d=d):
            for n in range(KV):
                rows = pl.ds(KVROWS * n, KVROWS)
                pltpu.make_async_copy(near.at[sources[d] & (NFAR - 1), rows, :], slot.at[d, rows, :], in_sem.at[d, n]).start()

        for m in range(NFAR):

            @pl.when(sources[d] == NFAR + m)
            def _(d=d, m=m):
                for n in range(KV):
                    load(d, n, m).start()


    def stores(n):
        rows, wide, narrow = pl.ds(HOME, MOVE), pl.ds(GROUP * HD * n, GROUP * HD), pl.ds(HD * n, HD)
        return [
            pltpu.make_async_copy(o_out.at[n % 2], out.at[rows, wide], out_sem.at[0, n % 2]),
            pltpu.make_async_copy(q_out.at[n % 2], dq.at[rows, wide], out_sem.at[1, n % 2]),
            pltpu.make_async_copy(k_out.at[n % 2], dk.at[rows, narrow], out_sem.at[2, n % 2]),
            pltpu.make_async_copy(v_out.at[n % 2], dv.at[rows, narrow], out_sem.at[3, n % 2]),
        ]

    zeros = jnp.zeros((S, HD), BF)
    lower = lax.broadcasted_iota(jnp.int32, (HD, HD), 0)
    across = lax.broadcasted_iota(jnp.int32, (HD, HD), 1)
    same = (lower & (S - 1)) == (across & (S - 1))
    ones = jnp.where((lower < S) == (across < S), 1.0, 0.0).astype(BF)

    def twice(x):
        return jnp.concatenate([jnp.concatenate([x, zeros], axis=1), jnp.concatenate([zeros, x], axis=1)], axis=0)

    def spread_heads(x):
        return jnp.concatenate([x[:S, :HD], x[S:, :HD], x[:S, HD:], x[S:, HD:]], axis=1)

    row = lax.broadcasted_iota(jnp.int32, (HD, 1), 0)
    column = lax.broadcasted_iota(jnp.int32, (1, HD), 1)
    shared = 6 * S
    for buf in (o_buf, q_buf, k_buf, v_buf):
        buf[shared:, :] = jnp.zeros((MOVE + S - shared, buf.shape[1]), F32)
    docs = range(NDOC)
    landing = [landings[d] for d in docs]
    shift = [landing[d] & (S - 1) for d in docs]
    first = [pl.multiple_of(landing[d] - shift[d], S) for d in docs]
    for n in range(KV):
        for d in docs:
            load(d, n).wait()
        base = KVROWS * n
        for half in (docs[: NDOC // 2], docs[NDOC // 2 :]):
            causal = {d: ((row - landing[d]) & (S - 1)) <= ((column - landing[d]) & (S - 1)) for d in half}
            square = {d: slot[d, base : base + 2 * S, :].astype(F32) for d in half}
            weights = {d: jnp.where(causal[d], square[d], 0.0) for d in half}
            grad = {d: square[d] - weights[d] for d in half}
            sums = {d: dot(grad[d].astype(BF), ones, NN) for d in half}
            attended = {d: dot(weights[d].T.astype(BF), twice(slot[d, base + 3 * S : base + 4 * S, :]), NN) for d in half}
            grad = {d: jnp.where(same, -sums[d], grad[d]).astype(BF) for d in half}
            query = {d: dot(grad[d], twice(slot[d, base + 2 * S : base + 3 * S, :]), NN) * SCALE for d in half}

            def put(buf, d, value):
                kept = lax.broadcasted_iota(jnp.int32, value.shape, 0) >= shift[d]
                pltpu.store(buf.at[pl.ds(first[d], S), :], value, mask=kept)
                pltpu.store(buf.at[pl.ds(first[d] + S, S), :], value, mask=jnp.logical_not(kept))

            for d in half:
                put(o_buf, d, spread_heads(attended[d]))
                put(q_buf, d, spread_heads(query[d]))
                put(k_buf, d, slot[d, base + 4 * S : base + 5 * S, :].astype(F32))
                put(v_buf, d, slot[d, base + 5 * S : base + 6 * S, :].astype(F32))
        if n >= 2:
            for copy in stores(n - 2):
                copy.wait()
        for buf, final in ((o_buf, o_out), (q_buf, q_out), (k_buf, k_out), (v_buf, v_out)):
            final[n % 2] = buf[:MOVE, :].astype(BF)
        for copy in stores(n):
            copy.start()
    for n in (KV - 2, KV - 1):
        for copy in stores(n):
            copy.wait()


def receive(sources, landings, near, far, outs):
    hbm = pl.BlockSpec(memory_space=pltpu.HBM)
    smem = pl.BlockSpec(memory_space=pltpu.SMEM)
    padded = MOVE + S
    wide, narrow = GROUP * HD, HD
    return pl.pallas_call(
        receive_kernel,
        out_shape=[jax.ShapeDtypeStruct(o.shape, o.dtype) for o in outs],
        in_specs=[smem, smem] + [hbm] * (1 + NFAR + 4),
        out_specs=[hbm] * 4,
        input_output_aliases={3 + NFAR + i: i for i in range(4)},
        scratch_shapes=[
            pltpu.VMEM((NDOC, KVROWS * KV, HD), BF),
            pltpu.VMEM((padded, wide), F32),
            pltpu.VMEM((padded, wide), F32),
            pltpu.VMEM((padded, narrow), F32),
            pltpu.VMEM((padded, narrow), F32),
            pltpu.VMEM((2, MOVE, wide), BF),
            pltpu.VMEM((2, MOVE, wide), BF),
            pltpu.VMEM((2, MOVE, narrow), BF),
            pltpu.VMEM((2, MOVE, narrow), BF),
            pltpu.SemaphoreType.DMA((NDOC, KV)),
            pltpu.SemaphoreType.DMA((4, 2)),
        ],
        cost_estimate=pl.CostEstimate(flops=4_000_000_000, bytes_accessed=10_000_000, transcendentals=0),
        name="receive",
    )(sources, landings, near, *far, *outs)


def placement(codes):
    valid = codes > 0
    rank = jnp.sum((valid[None, :] & (codes[None, :] < codes[:, None])).astype(jnp.int32), axis=1)
    order = jnp.arange(NDOC, dtype=jnp.int32)
    chosen = valid[None, :] & (rank[None, :] == order[:, None])
    sources = jnp.sum(jnp.where(chosen, jnp.arange(NSLOT, dtype=jnp.int32)[None, :], 0), axis=1)
    landings = jnp.sum(jnp.where(chosen, (codes - 1)[None, :], 0), axis=1)
    return sources, landings


def codes_of(meta):
    pairs = meta.astype(F32).astype(jnp.int32)
    return pairs[:, 0] * 32 + pairs[:, S]


def swap(x, axis, size, mask):
    return lax.ppermute(x, axis, [(i, i ^ mask) for i in range(size)])


def add(*terms):
    total = terms[0].astype(F32)
    for term in terms[1:]:
        total = total + term.astype(F32)
    return total


def shifts(pieces, axis, size):
    return [lax.ppermute(pieces(step), axis, [(i, (i + step) % size) for i in range(size)]) for step in range(1, size)]


def reduce_cores(layer_grad):
    grad = layer_grad.reshape(2, 4, 2, 4, 64, layer_grad.shape[-1])
    core = lax.axis_index("core")
    mine = lax.dynamic_index_in_dim(grad, core, 2, keepdims=False)
    other = lax.dynamic_index_in_dim(grad, 1 - core, 2, keepdims=False)
    return add(mine, swap(other, "core", 2, 1)).astype(BF)


def reduce_ring(part, axis, dim):
    place = lax.axis_index(axis)

    def block(step):
        return lax.dynamic_index_in_dim(part, (place + step) % 4, dim, keepdims=False)

    return add(block(0), *shifts(block, axis, 4)).astype(BF)


def after(value, *others):
    return lax.optimization_barrier((value, *others))[0]


FAR_ORDER = (0, 2, 4, 6, 5, 7, 3, 1)


def per_device(q, k, v, g, home_lengths, moved_lengths, moved_offsets, moved_owner, owner_offsets, layer_grad):
    core, z, yhi, me = lax.axis_index("core"), lax.axis_index("z"), lax.axis_index("yhi"), lax.axis_index(DP)
    apart = moved_owner ^ me
    goal = jnp.where(apart < NFAR, moved_owner & (NFAR - 1), apart)
    table = jnp.concatenate([moved_lengths, moved_offsets, goal, owner_offsets], axis=0)

    grad = layer_grad.reshape(8, 2, 256, layer_grad.shape[-1])
    other = lax.dynamic_index_in_dim(grad, 1 - core, 1, keepdims=False)
    mine = lax.dynamic_index_in_dim(grad, core, 1, keepdims=False)
    table, other = lax.optimization_barrier((table, other))
    near, *far = send(table, q, k, v, g)
    part = add(mine, swap(other, "core", 2, 1)).astype(BF).reshape(2, 4, 4, 64, -1)
    near = lax.all_to_all(near, ("z", "core"), split_axis=0, concat_axis=0, tiled=True)
    part_x = reduce_ring(part, "x", 1)
    outs = home(home_lengths, q, k, v, g)
    part_x, *outs = lax.optimization_barrier((part_x, *outs))
    needs = {3: (part,), 5: tuple(outs), 6: (part_x,)}
    for place, m in enumerate(FAR_ORDER):
        need = needs.get(place, ())
        if place >= 3:
            need = (far[FAR_ORDER[place - 3]], *need)
        payload = after(far[m], *need) if need else far[m]
        far[m] = lax.ppermute(payload, DP, [(i, i ^ (NFAR + m)) for i in range(NSLOT)])

    def z_block(step):
        return lax.dynamic_index_in_dim(part_x, (z + step) % 4, 1, keepdims=False)

    from_z = shifts(z_block, "z", 4)
    part_z = add(z_block(0), *from_z).astype(BF)
    kept = lax.dynamic_index_in_dim(part_z, yhi, 0, keepdims=False)
    given = lax.dynamic_index_in_dim(part_z, 1 - yhi, 0, keepdims=False)
    from_y = [lax.ppermute(given if mask & 1 else kept, ("ylo", "yhi"), [(i, i ^ mask) for i in range(4)]) for mask in (1, 2, 3)]
    total = add(kept, *from_y).astype(BF)
    held = [total, *shifts(lambda step: total, "z", 4)]

    meta = jnp.concatenate([near[:, KVROWS * KV, :], jnp.stack([f[KVROWS * KV, :] for f in far])], axis=0)
    sources, landings = placement(codes_of(meta))
    outs = receive(sources, landings, near, far, outs)
    held, outs = lax.optimization_barrier((held, outs))

    held = jnp.stack(held)
    half = jnp.concatenate([lax.dynamic_index_in_dim(held, (z - b) % 4, 0, keepdims=False) for b in range(4)], axis=0)
    twin = swap(half, "core", 2, 1)
    first = jnp.where(core == 0, half, twin)
    second = jnp.where(core == 0, twin, half)
    return (*outs, jnp.concatenate([first, second], axis=0).astype(F32))


def solution(mesh):
    fine = Mesh(mesh.devices.reshape(2, 4, 2, 2, 4), FINE)
    rows = P(FINE, None)
    return jax.shard_map(
        per_device,
        mesh=fine,
        in_specs=(rows,) * 9 + (P(DP, ("yhi", "x"), None, None),),
        out_specs=(rows, rows, rows, rows, P(("yhi", "x"), None)),
        check_vma=False,
    )
```

```python
import functools
import math

import jax
import jax.numpy as jnp
from jax import lax
from jax.experimental import pallas as pl
from jax.experimental.pallas import tpu as pltpu
from jax.sharding import Mesh
from jax.sharding import PartitionSpec as P

HD = 128
HOME = 384
S = 64
MOVE = 512
NDOC = 8
GROUP = 4
KV = 4
WIN = 80
NSLOT = 16
NFAR = 8
KVROWS = 6 * S
META = 8
SCALE = 1.0 / math.sqrt(HD)
EXP2_SCALE = SCALE * math.log2(math.e)
FINE = ("ylo", "z", "core", "yhi", "x")
DP = ("ylo", "z", "core")
BF = jnp.bfloat16
F32 = jnp.float32


def dot(a, b, dims):
    return lax.dot_general(a, b, (dims, ((), ())), preferred_element_type=F32)


NN = ((1,), (0,))
NT = ((1,), (1,))
TN = ((0,), (0,))


def heads_to_rows(x):
    return jnp.concatenate([x[:, HD * h : HD * (h + 1)] for h in range(GROUP)], axis=0)


def transposed_softmax(scores, allowed, filled=None):
    scores = jnp.where(allowed, scores * EXP2_SCALE, -1e30)
    highest = jnp.max(scores, axis=0, keepdims=True)
    exponent = jnp.exp2(scores - highest)
    inverse = 1.0 / jnp.sum(exponent, axis=0, keepdims=True)
    if filled is not None:
        inverse = jnp.where(filled, inverse, 0.0)
    return exponent * inverse


def send_kernel(table, q_hbm, k_hbm, v_hbm, g_hbm, *refs):
    near, far = refs[0], refs[1 : 1 + NFAR]
    q, k, v, g, slot, meta, in_sem, out_sem, meta_sem = refs[1 + NFAR :]
    chunk = 128
    pairs = ((q_hbm, q), (g_hbm, g), (k_hbm, k), (v_hbm, v))

    def load(a, b):
        source, target = pairs[a]
        return pltpu.make_async_copy(source.at[pl.ds(HOME + chunk * b, chunk), :], target.at[pl.ds(chunk * b, chunk), :], in_sem.at[a, b])

    for b in range(MOVE // chunk):
        for a in range(4):
            load(a, b).start()
    lane = lax.broadcasted_iota(jnp.int32, (META, HD), 1)
    for s in range(NSLOT):
        code = jnp.int32(0)
        for d in range(NDOC):
            code = code + jnp.where(table[2, d] == s, table[3, d] + 1, 0)
        meta[s] = jnp.where(lane < S, lax.shift_right_logical(code, 5), code & 31).astype(F32).astype(BF)

    body, tail = pl.ds(0, KVROWS * KV), pl.ds(KVROWS * KV, META)
    meta_copies = [pltpu.make_async_copy(meta.at[pl.ds(0, NFAR)], near.at[:, tail, :], meta_sem.at[NFAR])]
    meta_copies += [pltpu.make_async_copy(meta.at[NFAR + m], far[m].at[tail, :], meta_sem.at[m]) for m in range(NFAR)]
    for copy in meta_copies:
        copy.start()

    def store_near(d):
        return pltpu.make_async_copy(slot.at[d % 2], near.at[table[2, d] & (NFAR - 1), body, :], out_sem.at[d % 2])

    def store_far(d, m):
        return pltpu.make_async_copy(slot.at[d % 2], far[m].at[body, :], out_sem.at[d % 2])

    def store(d):
        @pl.when(table[2, d] < NFAR)
        def _():
            store_near(d).start()

        for m in range(NFAR):

            @pl.when(table[2, d] == NFAR + m)
            def _(m=m):
                store_far(d, m).start()

    same = (lax.broadcasted_iota(jnp.int32, (HD, HD), 0) & (S - 1)) == (lax.broadcasted_iota(jnp.int32, (HD, HD), 1) & (S - 1))
    loaded = -1
    for d in range(NDOC):
        last = min((S * d + WIN - 1) // chunk, MOVE // chunk - 1)
        while loaded < last:
            loaded += 1
            for a in range(4):
                load(a, loaded).wait()
        length, offset, landing = table[0, d], table[1, d], table[3, d]
        start = pl.multiple_of(jnp.minimum(lax.shift_right_logical(offset, 4) * 16, MOVE - WIN), 16)
        inside = (lax.broadcasted_iota(jnp.int32, (S, WIN), 0) - landing) & (S - 1)
        source = lax.broadcasted_iota(jnp.int32, (S, WIN), 1)
        pick = jnp.where((source - (offset - start) == inside) & (inside < length), 1.0, 0.0).astype(BF)
        key_place = (lax.broadcasted_iota(jnp.int32, (S, 1), 0) - landing) & (S - 1)
        query_place = (lax.broadcasted_iota(jnp.int32, (1, GROUP * S), 1) - landing) & (S - 1)
        filled = query_place < length
        allowed = key_place <= jnp.where(filled, query_place, -1)
        window = pl.ds(start, WIN)
        all_k = dot(pick, k[window, :], NN).astype(BF)
        all_v = dot(pick, v[window, :], NN).astype(BF)
        if d >= 2:
            store_far(d - 2, 0).wait()
        here = slot.at[d % 2]
        each = range(KV)
        wide = [slice(GROUP * HD * n, GROUP * HD * (n + 1)) for n in each]
        kd = [all_k[:, HD * n : HD * (n + 1)] for n in each]
        vd = [all_v[:, HD * n : HD * (n + 1)] for n in each]
        qs = [heads_to_rows(dot(pick, q[window, wide[n]], NN).astype(BF)) for n in each]
        gs = [heads_to_rows(dot(pick, g[window, wide[n]], NN).astype(BF)) for n in each]
        scores = [dot(kd[n], qs[n], NT) for n in each]
        logits = [dot(vd[n], gs[n], NT) for n in each]
        weights = [transposed_softmax(scores[n], allowed, filled) for n in each]
        delta = [jnp.sum(weights[n] * logits[n], axis=0, keepdims=True) for n in each]
        grad = [weights[n] * (logits[n] - delta[n]) for n in each]
        both = [jnp.concatenate([weights[n].astype(BF), grad[n].astype(BF)], axis=0) for n in each]
        summed = [dot(both[n], jnp.concatenate([gs[n], qs[n]], axis=1), NN) for n in each]
        for n in each:
            turned = jnp.concatenate([grad[n][:, :HD], grad[n][:, HD:]], axis=0).T
            square = jnp.concatenate([weights[n][:, :HD], weights[n][:, HD:]], axis=0) + jnp.where(same, 0.0, turned)
            base = KVROWS * n
            here[base : base + 2 * S, :] = square.astype(BF)
            here[base + 2 * S : base + 3 * S, :] = kd[n]
            here[base + 3 * S : base + 4 * S, :] = vd[n]
            here[base + 4 * S : base + 5 * S, :] = (summed[n][S:, HD:] * SCALE).astype(BF)
            here[base + 5 * S : base + 6 * S, :] = summed[n][:S, :HD].astype(BF)
        store(d)
    store_far(NDOC - 2, 0).wait()
    store_far(NDOC - 1, 0).wait()
    for copy in meta_copies:
        copy.wait()


def send(table, q, k, v, g):
    hbm = pl.BlockSpec(memory_space=pltpu.HBM)
    return pl.pallas_call(
        send_kernel,
        out_shape=[jax.ShapeDtypeStruct((NFAR, KVROWS * KV + META, HD), BF)] + [jax.ShapeDtypeStruct((KVROWS * KV + META, HD), BF)] * NFAR,
        in_specs=[pl.BlockSpec(memory_space=pltpu.SMEM)] + [hbm] * 4,
        out_specs=[hbm] * (1 + NFAR),
        scratch_shapes=[
            pltpu.VMEM((MOVE, KV * GROUP * HD), BF),
            pltpu.VMEM((MOVE, KV * HD), BF),
            pltpu.VMEM((MOVE, KV * HD), BF),
            pltpu.VMEM((MOVE, KV * GROUP * HD), BF),
            pltpu.VMEM((2, KVROWS * KV, HD), BF),
            pltpu.VMEM((NSLOT, META, HD), BF),
            pltpu.SemaphoreType.DMA((4, 4)),
            pltpu.SemaphoreType.DMA((2,)),
            pltpu.SemaphoreType.DMA((1 + NFAR,)),
        ],
        cost_estimate=pl.CostEstimate(flops=4_000_000_000, bytes_accessed=10_000_000, transcendentals=1_000_000),
        name="send",
    )(table, q, k, v, g)


def home_kernel(lengths, q, k, v, g, out, dq, dk, dv, acc_k, acc_v):
    block = 128
    ends = []
    total = jnp.int32(0)
    for i in range(6):
        total = total + lengths[0, i]
        ends.append(total)
    acc_k[...] = jnp.zeros_like(acc_k)
    acc_v[...] = jnp.zeros_like(acc_v)
    for b in range(3):
        low = max(0, block * (b - 1))
        span = block * (b + 1) - low
        rows = slice(block * b, block * (b + 1))
        keys = slice(low, low + span)
        position = block * b + (lax.broadcasted_iota(jnp.int32, (1, GROUP * block), 1) & (block - 1))
        start = jnp.zeros_like(position)
        for end in ends:
            start = jnp.where(position >= end, end, start)
        key_position = low + lax.broadcasted_iota(jnp.int32, (span, GROUP * block), 0)
        allowed = (key_position <= position) & (key_position >= start)
        qs, gs = heads_to_rows(q[rows, :]), heads_to_rows(g[rows, :])
        kb, vb = k[keys, :], v[keys, :]
        weights = transposed_softmax(dot(kb, qs, NT), allowed)
        logits = dot(vb, gs, NT)
        delta = jnp.sum(weights * logits, axis=0, keepdims=True)
        grad = (weights * (logits - delta)).astype(BF)
        weights = weights.astype(BF)
        acc_v[keys, :] += dot(weights, gs, NN)
        acc_k[keys, :] += dot(grad, qs, NN)
        turned_out = dot(vb, weights, TN)
        turned_dq = dot(kb, grad, TN) * SCALE
        for h in range(GROUP):
            lanes = slice(block * h, block * (h + 1))
            out[rows, HD * h : HD * (h + 1)] = turned_out[:, lanes].T.astype(BF)
            dq[rows, HD * h : HD * (h + 1)] = turned_dq[:, lanes].T.astype(BF)
    dk[...] = (acc_k[...] * SCALE).astype(BF)
    dv[...] = acc_v[...].astype(BF)


def home(lengths, q, k, v, g):
    total = q.shape[0]
    wide = pl.BlockSpec((HOME, GROUP * HD), lambda c: (0, c))
    narrow = pl.BlockSpec((HOME, HD), lambda c: (0, c))
    return pl.pallas_call(
        home_kernel,
        out_shape=[
            pltpu.HBM((total, KV * GROUP * HD), BF),
            pltpu.HBM((total, KV * GROUP * HD), BF),
            pltpu.HBM((total, KV * HD), BF),
            pltpu.HBM((total, KV * HD), BF),
        ],
        grid=(KV,),
        in_specs=[pl.BlockSpec(memory_space=pltpu.SMEM), wide, narrow, narrow, wide],
        out_specs=[wide, wide, narrow, narrow],
        scratch_shapes=[pltpu.VMEM((HOME, HD), F32), pltpu.VMEM((HOME, HD), F32)],
        cost_estimate=pl.CostEstimate(flops=10_000_000_000, bytes_accessed=10_000_000, transcendentals=2_000_000),
        name="home",
    )(lengths, q, k, v, g)


def receive_kernel(kvs, near, *refs):
    far = refs[:NFAR]
    out, dq, dk, dv = refs[NFAR + 4 : NFAR + 8]
    slot, o_buf, q_buf, k_buf, v_buf, o_out, q_out, k_out, v_out, meta, sources, landings, in_sem, out_sem, meta_sem = refs[NFAR + 8 :]
    tail = pl.ds(KVROWS * KV, META)
    meta_copies = [pltpu.make_async_copy(near.at[:, tail, :], meta.at[pl.ds(0, NFAR)], meta_sem.at[NFAR])]
    meta_copies += [pltpu.make_async_copy(far[m].at[tail, :], meta.at[NFAR + m], meta_sem.at[m]) for m in range(NFAR)]
    for copy in meta_copies:
        copy.start()
    for copy in meta_copies:
        copy.wait()
    lane = lax.broadcasted_iota(jnp.int32, (META, HD), 1)
    top = lax.broadcasted_iota(jnp.int32, (META, HD), 0) == 0
    factor = jnp.where(top & (lane == 0), 32.0, jnp.where(top & (lane == S), 1.0, 0.0))
    codes = [jnp.sum(meta[s].astype(F32) * factor).astype(jnp.int32) for s in range(NSLOT)]
    for s in range(NSLOT):
        rank = jnp.int32(0)
        for t in range(NSLOT):
            if t != s:
                rank = rank + jnp.where((codes[t] > 0) & (codes[t] < codes[s]), 1, 0)

        @pl.when(codes[s] > 0)
        def _(s=s, rank=rank):
            sources[rank] = jnp.int32(s)
            landings[rank] = codes[s] - 1


    def load(d, i, m=0):
        source, rows = pl.ds(KVROWS * kvs[i], KVROWS), pl.ds(KVROWS * i, KVROWS)
        return pltpu.make_async_copy(far[m].at[source, :], slot.at[d, rows, :], in_sem.at[d, i])

    def load_near(d, i):
        source, rows = pl.ds(KVROWS * kvs[i], KVROWS), pl.ds(KVROWS * i, KVROWS)
        return pltpu.make_async_copy(near.at[sources[d] & (NFAR - 1), source, :], slot.at[d, rows, :], in_sem.at[d, i])

    for d in range(NDOC):

        @pl.when(sources[d] < NFAR)
        def _(d=d):
            for i in range(len(kvs)):
                load_near(d, i).start()

        for m in range(NFAR):

            @pl.when(sources[d] == NFAR + m)
            def _(d=d, m=m):
                for i in range(len(kvs)):
                    load(d, i, m).start()


    def stores(i):
        n = kvs[i]
        rows, wide, narrow = pl.ds(HOME, MOVE), pl.ds(GROUP * HD * n, GROUP * HD), pl.ds(HD * n, HD)
        return [
            pltpu.make_async_copy(o_out.at[i % 2], out.at[rows, wide], out_sem.at[0, i % 2]),
            pltpu.make_async_copy(q_out.at[i % 2], dq.at[rows, wide], out_sem.at[1, i % 2]),
            pltpu.make_async_copy(k_out.at[i % 2], dk.at[rows, narrow], out_sem.at[2, i % 2]),
            pltpu.make_async_copy(v_out.at[i % 2], dv.at[rows, narrow], out_sem.at[3, i % 2]),
        ]

    zeros = jnp.zeros((S, HD), BF)
    lower = lax.broadcasted_iota(jnp.int32, (HD, HD), 0)
    across = lax.broadcasted_iota(jnp.int32, (HD, HD), 1)
    same = (lower & (S - 1)) == (across & (S - 1))
    ones = jnp.where((lower < S) == (across < S), 1.0, 0.0).astype(BF)

    def twice(x):
        return jnp.concatenate([jnp.concatenate([x, zeros], axis=1), jnp.concatenate([zeros, x], axis=1)], axis=0)

    def spread_heads(x):
        return jnp.concatenate([x[:S, :HD], x[S:, :HD], x[:S, HD:], x[S:, HD:]], axis=1)

    row = lax.broadcasted_iota(jnp.int32, (HD, 1), 0)
    column = lax.broadcasted_iota(jnp.int32, (1, HD), 1)
    shared = 6 * S
    for buf in (o_buf, q_buf, k_buf, v_buf):
        buf[shared:, :] = jnp.zeros((MOVE + S - shared, buf.shape[1]), F32)
    docs = range(NDOC)
    landing = [landings[d] for d in docs]
    shift = [landing[d] & (S - 1) for d in docs]
    first = [pl.multiple_of(landing[d] - shift[d], S) for d in docs]
    for i in range(len(kvs)):
        for d in docs:
            load(d, i).wait()
        base = KVROWS * i
        for half in (docs[: NDOC // 2], docs[NDOC // 2 :]):
            causal = {d: ((row - landing[d]) & (S - 1)) <= ((column - landing[d]) & (S - 1)) for d in half}
            square = {d: slot[d, base : base + 2 * S, :].astype(F32) for d in half}
            weights = {d: jnp.where(causal[d], square[d], 0.0) for d in half}
            grad = {d: square[d] - weights[d] for d in half}
            sums = {d: dot(grad[d].astype(BF), ones, NN) for d in half}
            attended = {d: dot(weights[d].T.astype(BF), twice(slot[d, base + 3 * S : base + 4 * S, :]), NN) for d in half}
            grad = {d: jnp.where(same, -sums[d], grad[d]).astype(BF) for d in half}
            query = {d: dot(grad[d], twice(slot[d, base + 2 * S : base + 3 * S, :]), NN) * SCALE for d in half}

            def put(buf, d, value):
                kept = lax.broadcasted_iota(jnp.int32, value.shape, 0) >= shift[d]
                pltpu.store(buf.at[pl.ds(first[d], S), :], value, mask=kept)
                pltpu.store(buf.at[pl.ds(first[d] + S, S), :], value, mask=jnp.logical_not(kept))

            for d in half:
                put(o_buf, d, spread_heads(attended[d]))
                put(q_buf, d, spread_heads(query[d]))
                put(k_buf, d, slot[d, base + 4 * S : base + 5 * S, :].astype(F32))
                put(v_buf, d, slot[d, base + 5 * S : base + 6 * S, :].astype(F32))
        if i >= 2:
            for copy in stores(i - 2):
                copy.wait()
        for buf, final in ((o_buf, o_out), (q_buf, q_out), (k_buf, k_out), (v_buf, v_out)):
            final[i % 2] = buf[:MOVE, :].astype(BF)
        for copy in stores(i):
            copy.start()
    for i in range(max(0, len(kvs) - 2), len(kvs)):
        for copy in stores(i):
            copy.wait()


def receive(near, far, outs, kvs):
    hbm = pl.BlockSpec(memory_space=pltpu.HBM)
    padded = MOVE + S
    wide, narrow = GROUP * HD, HD
    return pl.pallas_call(
        functools.partial(receive_kernel, kvs),
        out_shape=[jax.ShapeDtypeStruct(o.shape, o.dtype) for o in outs],
        in_specs=[pl.BlockSpec(memory_space=pl.ANY)] + [hbm] * (NFAR + 4),
        out_specs=[hbm] * 4,
        input_output_aliases={1 + NFAR + i: i for i in range(4)},
        scratch_shapes=[
            pltpu.VMEM((NDOC, KVROWS * len(kvs), HD), BF),
            pltpu.VMEM((padded, wide), F32),
            pltpu.VMEM((padded, wide), F32),
            pltpu.VMEM((padded, narrow), F32),
            pltpu.VMEM((padded, narrow), F32),
            pltpu.VMEM((2, MOVE, wide), BF),
            pltpu.VMEM((2, MOVE, wide), BF),
            pltpu.VMEM((2, MOVE, narrow), BF),
            pltpu.VMEM((2, MOVE, narrow), BF),
            pltpu.VMEM((NSLOT, META, HD), BF),
            pltpu.SMEM((NDOC,), jnp.int32),
            pltpu.SMEM((NDOC,), jnp.int32),
            pltpu.SemaphoreType.DMA((NDOC, len(kvs))),
            pltpu.SemaphoreType.DMA((4, 2)),
            pltpu.SemaphoreType.DMA((1 + NFAR,)),
        ],
        cost_estimate=pl.CostEstimate(flops=1_000_000_000 * len(kvs), bytes_accessed=2_500_000 * len(kvs), transcendentals=0),
        name="receive",
    )(near, *far, *outs)


def swap(x, axis, size, mask):
    return lax.ppermute(x, axis, [(i, i ^ mask) for i in range(size)])


def add(*terms):
    total = terms[0].astype(F32)
    for term in terms[1:]:
        total = total + term.astype(F32)
    return total


def shifts(pieces, axis, size):
    return [lax.ppermute(pieces(step), axis, [(i, (i + step) % size) for i in range(size)]) for step in range(1, size)]


def reduce_cores(layer_grad):
    grad = layer_grad.reshape(2, 4, 2, 4, 64, layer_grad.shape[-1])
    core = lax.axis_index("core")
    mine = lax.dynamic_index_in_dim(grad, core, 2, keepdims=False)
    other = lax.dynamic_index_in_dim(grad, 1 - core, 2, keepdims=False)
    return add(mine, swap(other, "core", 2, 1)).astype(BF)


def reduce_ring(part, axis, dim):
    place = lax.axis_index(axis)

    def block(step):
        return lax.dynamic_index_in_dim(part, (place + step) % 4, dim, keepdims=False)

    return add(block(0), *shifts(block, axis, 4)).astype(BF)


def after(value, *others):
    return lax.optimization_barrier((value, *others))[0]


FAR_ORDER = (0, 2, 4, 6, 5, 7, 3, 1)


def per_device(q, k, v, g, home_lengths, moved_lengths, moved_offsets, moved_owner, owner_offsets, layer_grad):
    core, z, yhi, me = lax.axis_index("core"), lax.axis_index("z"), lax.axis_index("yhi"), lax.axis_index(DP)
    apart = moved_owner ^ me
    goal = jnp.where(apart < NFAR, moved_owner & (NFAR - 1), apart)
    table = jnp.concatenate([moved_lengths, moved_offsets, goal, owner_offsets], axis=0)

    grad = layer_grad.reshape(8, 2, 256, layer_grad.shape[-1])
    other = lax.dynamic_index_in_dim(grad, 1 - core, 1, keepdims=False)
    mine = lax.dynamic_index_in_dim(grad, core, 1, keepdims=False)
    table, other = lax.optimization_barrier((table, other))
    near, *far = send(table, q, k, v, g)
    part = add(mine, swap(other, "core", 2, 1)).astype(BF).reshape(2, 4, 256, -1)
    near = lax.all_to_all(near, ("z", "core"), split_axis=0, concat_axis=0, tiled=True)
    part_x = reduce_ring(part, "x", 1).reshape(2, 4, 64, -1)
    outs = home(home_lengths, q, k, v, g)
    part_x, *outs = lax.optimization_barrier((part_x, *outs))
    needs = {3: (part,), 5: tuple(outs), 6: (part_x,)}
    for place, m in enumerate(FAR_ORDER):
        need = needs.get(place, ())
        if place >= 3:
            need = (far[FAR_ORDER[place - 3]], *need)
        payload = after(far[m], *need) if need else far[m]
        far[m] = lax.ppermute(payload, DP, [(i, i ^ (NFAR + m)) for i in range(NSLOT)])

    def z_block(step):
        return lax.dynamic_index_in_dim(part_x, (z + step) % 4, 1, keepdims=False)

    from_z = shifts(z_block, "z", 4)
    part_z = add(z_block(0), *from_z).astype(BF)
    kept = lax.dynamic_index_in_dim(part_z, yhi, 0, keepdims=False)
    given = lax.dynamic_index_in_dim(part_z, 1 - yhi, 0, keepdims=False)
    from_y = [lax.ppermute(given if mask & 1 else kept, ("ylo", "yhi"), [(i, i ^ mask) for i in range(4)]) for mask in (1, 2, 3)]
    outs = receive(near, far, outs, (0, 1))
    from_y, outs = lax.optimization_barrier((from_y, outs))
    total = add(kept, *from_y).astype(BF)
    held = [total, *shifts(lambda step: total, "z", 4)]
    *outs, total = lax.optimization_barrier((*outs, total))
    outs = receive(near, far, outs, (2, 3))
    held, outs = lax.optimization_barrier((held, outs))


    held = jnp.stack(held)
    half = jnp.concatenate([lax.dynamic_index_in_dim(held, (z - b) % 4, 0, keepdims=False) for b in range(4)], axis=0)
    twin = swap(half, "core", 2, 1)
    first = jnp.where(core == 0, half, twin)
    second = jnp.where(core == 0, twin, half)
    return (*outs, jnp.concatenate([first, second], axis=0).astype(F32))


def solution(mesh):
    fine = Mesh(mesh.devices.reshape(2, 4, 2, 2, 4), FINE)
    rows = P(FINE, None)
    return jax.shard_map(
        per_device,
        mesh=fine,
        in_specs=(rows,) * 9 + (P(DP, ("yhi", "x"), None, None),),
        out_specs=(rows, rows, rows, rows, P(("yhi", "x"), None)),
        check_vma=False,
    )
```

```python
import functools
import math

import jax
import jax.numpy as jnp
from jax import lax
from jax.experimental import pallas as pl
from jax.experimental.pallas import tpu as pltpu
from jax.sharding import Mesh
from jax.sharding import PartitionSpec as P

HD = 128
HOME = 384
S = 64
MOVE = 512
NDOC = 8
GROUP = 4
KV = 4
WIN = 80
NSLOT = 16
NFAR = 8
KVROWS = 6 * S
META = 8
SCALE = 1.0 / math.sqrt(HD)
EXP2_SCALE = SCALE * math.log2(math.e)
FINE = ("ylo", "z", "core", "yhi", "x")
DP = ("ylo", "z", "core")
BF = jnp.bfloat16
F32 = jnp.float32


def dot(a, b, dims):
    return lax.dot_general(a, b, (dims, ((), ())), preferred_element_type=F32)


NN = ((1,), (0,))
NT = ((1,), (1,))
TN = ((0,), (0,))


def heads_to_rows(x):
    return jnp.concatenate([x[:, HD * h : HD * (h + 1)] for h in range(GROUP)], axis=0)


def transposed_softmax(scores, allowed, filled=None):
    scores = jnp.where(allowed, scores * EXP2_SCALE, -1e30)
    highest = jnp.max(scores, axis=0, keepdims=True)
    exponent = jnp.exp2(scores - highest)
    inverse = 1.0 / jnp.sum(exponent, axis=0, keepdims=True)
    if filled is not None:
        inverse = jnp.where(filled, inverse, 0.0)
    return exponent * inverse


def send_kernel(table, q_hbm, k_hbm, v_hbm, g_hbm, *refs):
    near, far = refs[0], refs[1 : 1 + NFAR]
    q, k, v, g, slot, meta, in_sem, out_sem, meta_sem = refs[1 + NFAR :]
    chunk = 128
    pairs = ((q_hbm, q), (g_hbm, g), (k_hbm, k), (v_hbm, v))

    def load(a, b):
        source, target = pairs[a]
        return pltpu.make_async_copy(source.at[pl.ds(HOME + chunk * b, chunk), :], target.at[pl.ds(chunk * b, chunk), :], in_sem.at[a, b])

    for b in range(MOVE // chunk):
        for a in range(4):
            load(a, b).start()
    lane = lax.broadcasted_iota(jnp.int32, (META, HD), 1)
    for s in range(NSLOT):
        code = jnp.int32(0)
        for d in range(NDOC):
            code = code + jnp.where(table[2, d] == s, table[3, d] + 1, 0)
        meta[s] = jnp.where(lane < S, lax.shift_right_logical(code, 5), code & 31).astype(F32).astype(BF)

    body, tail = pl.ds(0, KVROWS * KV), pl.ds(KVROWS * KV, META)
    meta_copies = [pltpu.make_async_copy(meta.at[pl.ds(0, NFAR)], near.at[:, tail, :], meta_sem.at[NFAR])]
    meta_copies += [pltpu.make_async_copy(meta.at[NFAR + m], far[m].at[tail, :], meta_sem.at[m]) for m in range(NFAR)]
    for copy in meta_copies:
        copy.start()

    def store_near(d):
        return pltpu.make_async_copy(slot.at[d % 2], near.at[table[2, d] & (NFAR - 1), body, :], out_sem.at[d % 2])

    def store_far(d, m):
        return pltpu.make_async_copy(slot.at[d % 2], far[m].at[body, :], out_sem.at[d % 2])

    def store(d):
        @pl.when(table[2, d] < NFAR)
        def _():
            store_near(d).start()

        for m in range(NFAR):

            @pl.when(table[2, d] == NFAR + m)
            def _(m=m):
                store_far(d, m).start()

    same = (lax.broadcasted_iota(jnp.int32, (HD, HD), 0) & (S - 1)) == (lax.broadcasted_iota(jnp.int32, (HD, HD), 1) & (S - 1))
    loaded = -1
    for d in range(NDOC):
        last = min((S * d + WIN - 1) // chunk, MOVE // chunk - 1)
        while loaded < last:
            loaded += 1
            for a in range(4):
                load(a, loaded).wait()
        length, offset, landing = table[0, d], table[1, d], table[3, d]
        start = pl.multiple_of(jnp.minimum(lax.shift_right_logical(offset, 4) * 16, MOVE - WIN), 16)
        inside = (lax.broadcasted_iota(jnp.int32, (S, WIN), 0) - landing) & (S - 1)
        source = lax.broadcasted_iota(jnp.int32, (S, WIN), 1)
        pick = jnp.where((source - (offset - start) == inside) & (inside < length), 1.0, 0.0).astype(BF)
        key_place = (lax.broadcasted_iota(jnp.int32, (S, 1), 0) - landing) & (S - 1)
        query_place = (lax.broadcasted_iota(jnp.int32, (1, GROUP * S), 1) - landing) & (S - 1)
        filled = query_place < length
        allowed = key_place <= jnp.where(filled, query_place, -1)
        window = pl.ds(start, WIN)
        all_k = dot(pick, k[window, :], NN).astype(BF)
        all_v = dot(pick, v[window, :], NN).astype(BF)
        if d >= 2:
            store_far(d - 2, 0).wait()
        here = slot.at[d % 2]
        each = range(KV)
        wide = [slice(GROUP * HD * n, GROUP * HD * (n + 1)) for n in each]
        kd = [all_k[:, HD * n : HD * (n + 1)] for n in each]
        vd = [all_v[:, HD * n : HD * (n + 1)] for n in each]
        qs = [heads_to_rows(dot(pick, q[window, wide[n]], NN).astype(BF)) for n in each]
        gs = [heads_to_rows(dot(pick, g[window, wide[n]], NN).astype(BF)) for n in each]
        scores = [dot(kd[n], qs[n], NT) for n in each]
        logits = [dot(vd[n], gs[n], NT) for n in each]
        weights = [transposed_softmax(scores[n], allowed, filled) for n in each]
        delta = [jnp.sum(weights[n] * logits[n], axis=0, keepdims=True) for n in each]
        grad = [weights[n] * (logits[n] - delta[n]) for n in each]
        both = [jnp.concatenate([weights[n].astype(BF), grad[n].astype(BF)], axis=0) for n in each]
        summed = [dot(both[n], jnp.concatenate([gs[n], qs[n]], axis=1), NN) for n in each]
        for n in each:
            turned = jnp.concatenate([grad[n][:, :HD], grad[n][:, HD:]], axis=0).T
            square = jnp.concatenate([weights[n][:, :HD], weights[n][:, HD:]], axis=0) + jnp.where(same, 0.0, turned)
            base = KVROWS * n
            here[base : base + 2 * S, :] = square.astype(BF)
            here[base + 2 * S : base + 3 * S, :] = kd[n]
            here[base + 3 * S : base + 4 * S, :] = vd[n]
            here[base + 4 * S : base + 5 * S, :] = (summed[n][S:, HD:] * SCALE).astype(BF)
            here[base + 5 * S : base + 6 * S, :] = summed[n][:S, :HD].astype(BF)
        store(d)
    store_far(NDOC - 2, 0).wait()
    store_far(NDOC - 1, 0).wait()
    for copy in meta_copies:
        copy.wait()


def send(table, q, k, v, g):
    hbm = pl.BlockSpec(memory_space=pltpu.HBM)
    return pl.pallas_call(
        send_kernel,
        out_shape=[jax.ShapeDtypeStruct((NFAR, KVROWS * KV + META, HD), BF)] + [jax.ShapeDtypeStruct((KVROWS * KV + META, HD), BF)] * NFAR,
        in_specs=[pl.BlockSpec(memory_space=pltpu.SMEM)] + [hbm] * 4,
        out_specs=[hbm] * (1 + NFAR),
        scratch_shapes=[
            pltpu.VMEM((MOVE, KV * GROUP * HD), BF),
            pltpu.VMEM((MOVE, KV * HD), BF),
            pltpu.VMEM((MOVE, KV * HD), BF),
            pltpu.VMEM((MOVE, KV * GROUP * HD), BF),
            pltpu.VMEM((2, KVROWS * KV, HD), BF),
            pltpu.VMEM((NSLOT, META, HD), BF),
            pltpu.SemaphoreType.DMA((4, 4)),
            pltpu.SemaphoreType.DMA((2,)),
            pltpu.SemaphoreType.DMA((1 + NFAR,)),
        ],
        cost_estimate=pl.CostEstimate(flops=4_000_000_000, bytes_accessed=10_000_000, transcendentals=1_000_000),
        name="send",
    )(table, q, k, v, g)


def home_kernel(lengths, q, k, v, g, out, dq, dk, dv, acc_k, acc_v):
    block = 128
    ends = []
    total = jnp.int32(0)
    for i in range(6):
        total = total + lengths[0, i]
        ends.append(total)
    acc_k[...] = jnp.zeros_like(acc_k)
    acc_v[...] = jnp.zeros_like(acc_v)
    for b in range(3):
        low = max(0, block * (b - 1))
        span = block * (b + 1) - low
        rows = slice(block * b, block * (b + 1))
        keys = slice(low, low + span)
        position = block * b + (lax.broadcasted_iota(jnp.int32, (1, GROUP * block), 1) & (block - 1))
        start = jnp.zeros_like(position)
        for end in ends:
            start = jnp.where(position >= end, end, start)
        key_position = low + lax.broadcasted_iota(jnp.int32, (span, GROUP * block), 0)
        allowed = (key_position <= position) & (key_position >= start)
        qs, gs = heads_to_rows(q[rows, :]), heads_to_rows(g[rows, :])
        kb, vb = k[keys, :], v[keys, :]
        weights = transposed_softmax(dot(kb, qs, NT), allowed)
        logits = dot(vb, gs, NT)
        delta = jnp.sum(weights * logits, axis=0, keepdims=True)
        grad = (weights * (logits - delta)).astype(BF)
        weights = weights.astype(BF)
        acc_v[keys, :] += dot(weights, gs, NN)
        acc_k[keys, :] += dot(grad, qs, NN)
        turned_out = dot(vb, weights, TN)
        turned_dq = dot(kb, grad, TN) * SCALE
        for h in range(GROUP):
            lanes = slice(block * h, block * (h + 1))
            out[rows, HD * h : HD * (h + 1)] = turned_out[:, lanes].T.astype(BF)
            dq[rows, HD * h : HD * (h + 1)] = turned_dq[:, lanes].T.astype(BF)
    dk[...] = (acc_k[...] * SCALE).astype(BF)
    dv[...] = acc_v[...].astype(BF)


def home(lengths, q, k, v, g):
    total = q.shape[0]
    wide = pl.BlockSpec((HOME, GROUP * HD), lambda c: (0, c))
    narrow = pl.BlockSpec((HOME, HD), lambda c: (0, c))
    return pl.pallas_call(
        home_kernel,
        out_shape=[
            pltpu.HBM((total, KV * GROUP * HD), BF),
            pltpu.HBM((total, KV * GROUP * HD), BF),
            pltpu.HBM((total, KV * HD), BF),
            pltpu.HBM((total, KV * HD), BF),
        ],
        grid=(KV,),
        in_specs=[pl.BlockSpec(memory_space=pltpu.SMEM), wide, narrow, narrow, wide],
        out_specs=[wide, wide, narrow, narrow],
        scratch_shapes=[pltpu.VMEM((HOME, HD), F32), pltpu.VMEM((HOME, HD), F32)],
        cost_estimate=pl.CostEstimate(flops=10_000_000_000, bytes_accessed=10_000_000, transcendentals=2_000_000),
        name="home",
    )(lengths, q, k, v, g)


def receive_kernel(kvs, near, *refs):
    far = refs[:NFAR]
    out, dq, dk, dv = refs[NFAR + 4 : NFAR + 8]
    slot, o_buf, q_buf, k_buf, v_buf, o_out, q_out, k_out, v_out, meta, sources, landings, in_sem, out_sem, meta_sem = refs[NFAR + 8 :]
    tail = pl.ds(KVROWS * KV, META)
    meta_copies = [pltpu.make_async_copy(near.at[:, tail, :], meta.at[pl.ds(0, NFAR)], meta_sem.at[NFAR])]
    meta_copies += [pltpu.make_async_copy(far[m].at[tail, :], meta.at[NFAR + m], meta_sem.at[m]) for m in range(NFAR)]
    for copy in meta_copies:
        copy.start()
    for copy in meta_copies:
        copy.wait()
    lane = lax.broadcasted_iota(jnp.int32, (META, HD), 1)
    top = lax.broadcasted_iota(jnp.int32, (META, HD), 0) == 0
    factor = jnp.where(top & (lane == 0), 32.0, jnp.where(top & (lane == S), 1.0, 0.0))
    codes = [jnp.sum(meta[s].astype(F32) * factor).astype(jnp.int32) for s in range(NSLOT)]
    for s in range(NSLOT):
        rank = jnp.int32(0)
        for t in range(NSLOT):
            if t != s:
                rank = rank + jnp.where((codes[t] > 0) & (codes[t] < codes[s]), 1, 0)

        @pl.when(codes[s] > 0)
        def _(s=s, rank=rank):
            sources[rank] = jnp.int32(s)
            landings[rank] = codes[s] - 1


    def load(d, i, m=0):
        source, rows = pl.ds(KVROWS * kvs[i], KVROWS), pl.ds(KVROWS * i, KVROWS)
        return pltpu.make_async_copy(far[m].at[source, :], slot.at[d, rows, :], in_sem.at[d, i])

    def load_near(d, i):
        source, rows = pl.ds(KVROWS * kvs[i], KVROWS), pl.ds(KVROWS * i, KVROWS)
        return pltpu.make_async_copy(near.at[sources[d] & (NFAR - 1), source, :], slot.at[d, rows, :], in_sem.at[d, i])

    for d in range(NDOC):

        @pl.when(sources[d] < NFAR)
        def _(d=d):
            for i in range(len(kvs)):
                load_near(d, i).start()

        for m in range(NFAR):

            @pl.when(sources[d] == NFAR + m)
            def _(d=d, m=m):
                for i in range(len(kvs)):
                    load(d, i, m).start()


    def stores(i):
        n = kvs[i]
        rows, wide, narrow = pl.ds(HOME, MOVE), pl.ds(GROUP * HD * n, GROUP * HD), pl.ds(HD * n, HD)
        return [
            pltpu.make_async_copy(o_out.at[i % 2], out.at[rows, wide], out_sem.at[0, i % 2]),
            pltpu.make_async_copy(q_out.at[i % 2], dq.at[rows, wide], out_sem.at[1, i % 2]),
            pltpu.make_async_copy(k_out.at[i % 2], dk.at[rows, narrow], out_sem.at[2, i % 2]),
            pltpu.make_async_copy(v_out.at[i % 2], dv.at[rows, narrow], out_sem.at[3, i % 2]),
        ]

    zeros = jnp.zeros((S, HD), BF)
    lower = lax.broadcasted_iota(jnp.int32, (HD, HD), 0)
    across = lax.broadcasted_iota(jnp.int32, (HD, HD), 1)
    same = (lower & (S - 1)) == (across & (S - 1))
    ones = jnp.where((lower < S) == (across < S), 1.0, 0.0).astype(BF)

    def twice(x):
        return jnp.concatenate([jnp.concatenate([x, zeros], axis=1), jnp.concatenate([zeros, x], axis=1)], axis=0)

    def spread_heads(x):
        return jnp.concatenate([x[:S, :HD], x[S:, :HD], x[:S, HD:], x[S:, HD:]], axis=1)

    row = lax.broadcasted_iota(jnp.int32, (HD, 1), 0)
    column = lax.broadcasted_iota(jnp.int32, (1, HD), 1)
    shared = 6 * S
    for buf in (o_buf, q_buf, k_buf, v_buf):
        buf[shared:, :] = jnp.zeros((MOVE + S - shared, buf.shape[1]), F32)
    docs = range(NDOC)
    landing = [landings[d] for d in docs]
    shift = [landing[d] & (S - 1) for d in docs]
    first = [pl.multiple_of(landing[d] - shift[d], S) for d in docs]
    for i in range(len(kvs)):
        for d in docs:
            load(d, i).wait()
        base = KVROWS * i
        for half in (docs[: NDOC // 2], docs[NDOC // 2 :]):
            causal = {d: ((row - landing[d]) & (S - 1)) <= ((column - landing[d]) & (S - 1)) for d in half}
            square = {d: slot[d, base : base + 2 * S, :].astype(F32) for d in half}
            weights = {d: jnp.where(causal[d], square[d], 0.0) for d in half}
            grad = {d: square[d] - weights[d] for d in half}
            sums = {d: dot(grad[d].astype(BF), ones, NN) for d in half}
            attended = {d: dot(weights[d].T.astype(BF), twice(slot[d, base + 3 * S : base + 4 * S, :]), NN) for d in half}
            grad = {d: jnp.where(same, -sums[d], grad[d]).astype(BF) for d in half}
            query = {d: dot(grad[d], twice(slot[d, base + 2 * S : base + 3 * S, :]), NN) * SCALE for d in half}

            def put(buf, d, value):
                kept = lax.broadcasted_iota(jnp.int32, value.shape, 0) >= shift[d]
                pltpu.store(buf.at[pl.ds(first[d], S), :], value, mask=kept)
                pltpu.store(buf.at[pl.ds(first[d] + S, S), :], value, mask=jnp.logical_not(kept))

            for d in half:
                put(o_buf, d, spread_heads(attended[d]))
                put(q_buf, d, spread_heads(query[d]))
                put(k_buf, d, slot[d, base + 4 * S : base + 5 * S, :].astype(F32))
                put(v_buf, d, slot[d, base + 5 * S : base + 6 * S, :].astype(F32))
        if i >= 2:
            for copy in stores(i - 2):
                copy.wait()
        for buf, final in ((o_buf, o_out), (q_buf, q_out), (k_buf, k_out), (v_buf, v_out)):
            final[i % 2] = buf[:MOVE, :].astype(BF)
        for copy in stores(i):
            copy.start()
    for i in range(max(0, len(kvs) - 2), len(kvs)):
        for copy in stores(i):
            copy.wait()


def receive(near, far, outs, kvs):
    hbm = pl.BlockSpec(memory_space=pltpu.HBM)
    padded = MOVE + S
    wide, narrow = GROUP * HD, HD
    return pl.pallas_call(
        functools.partial(receive_kernel, kvs),
        out_shape=[jax.ShapeDtypeStruct(o.shape, o.dtype) for o in outs],
        in_specs=[pl.BlockSpec(memory_space=pl.ANY)] + [hbm] * (NFAR + 4),
        out_specs=[hbm] * 4,
        input_output_aliases={1 + NFAR + i: i for i in range(4)},
        scratch_shapes=[
            pltpu.VMEM((NDOC, KVROWS * len(kvs), HD), BF),
            pltpu.VMEM((padded, wide), F32),
            pltpu.VMEM((padded, wide), F32),
            pltpu.VMEM((padded, narrow), F32),
            pltpu.VMEM((padded, narrow), F32),
            pltpu.VMEM((2, MOVE, wide), BF),
            pltpu.VMEM((2, MOVE, wide), BF),
            pltpu.VMEM((2, MOVE, narrow), BF),
            pltpu.VMEM((2, MOVE, narrow), BF),
            pltpu.VMEM((NSLOT, META, HD), BF),
            pltpu.SMEM((NDOC,), jnp.int32),
            pltpu.SMEM((NDOC,), jnp.int32),
            pltpu.SemaphoreType.DMA((NDOC, len(kvs))),
            pltpu.SemaphoreType.DMA((4, 2)),
            pltpu.SemaphoreType.DMA((1 + NFAR,)),
        ],
        cost_estimate=pl.CostEstimate(flops=1_000_000_000 * len(kvs), bytes_accessed=2_500_000 * len(kvs), transcendentals=0),
        name="receive",
    )(near, *far, *outs)


def swap(x, axis, size, mask):
    return lax.ppermute(x, axis, [(i, i ^ mask) for i in range(size)])


def add(*terms):
    total = terms[0].astype(F32)
    for term in terms[1:]:
        total = total + term.astype(F32)
    return total


def shifts(pieces, axis, size):
    return [lax.ppermute(pieces(step), axis, [(i, (i + step) % size) for i in range(size)]) for step in range(1, size)]


def reduce_cores(layer_grad):
    grad = layer_grad.reshape(2, 4, 2, 4, 64, layer_grad.shape[-1])
    core = lax.axis_index("core")
    mine = lax.dynamic_index_in_dim(grad, core, 2, keepdims=False)
    other = lax.dynamic_index_in_dim(grad, 1 - core, 2, keepdims=False)
    return add(mine, swap(other, "core", 2, 1)).astype(BF)


def reduce_ring(part, axis, dim):
    place = lax.axis_index(axis)

    def block(step):
        return lax.dynamic_index_in_dim(part, (place + step) % 4, dim, keepdims=False)

    return add(block(0), *shifts(block, axis, 4)).astype(BF)


def after(value, *others):
    return lax.optimization_barrier((value, *others))[0]


FAR_ORDER = (0, 2, 4, 6, 5, 7, 3, 1)


def per_device(q, k, v, g, home_lengths, moved_lengths, moved_offsets, moved_owner, owner_offsets, layer_grad):
    core, z, yhi, me = lax.axis_index("core"), lax.axis_index("z"), lax.axis_index("yhi"), lax.axis_index(DP)
    apart = moved_owner ^ me
    goal = jnp.where(apart < NFAR, moved_owner & (NFAR - 1), apart)
    table = jnp.concatenate([moved_lengths, moved_offsets, goal, owner_offsets], axis=0)

    grad = layer_grad.reshape(8, 2, 256, layer_grad.shape[-1])
    other = lax.dynamic_index_in_dim(grad, 1 - core, 1, keepdims=False)
    mine = lax.dynamic_index_in_dim(grad, core, 1, keepdims=False)
    near, *far = send(table, q, k, v, g)
    part = add(mine, swap(other, "core", 2, 1)).astype(BF).reshape(2, 4, 256, -1)
    near = lax.all_to_all(near, ("z", "core"), split_axis=0, concat_axis=0, tiled=True)
    part_x = reduce_ring(part, "x", 1).reshape(2, 4, 64, -1)
    outs = home(home_lengths, q, k, v, g)
    part_x, *outs = lax.optimization_barrier((part_x, *outs))
    needs = {3: (part,), 5: tuple(outs), 6: (part_x,)}
    for place, m in enumerate(FAR_ORDER):
        need = needs.get(place, ())
        if place >= 3:
            need = (far[FAR_ORDER[place - 3]], *need)
        payload = after(far[m], *need) if need else far[m]
        far[m] = lax.ppermute(payload, DP, [(i, i ^ (NFAR + m)) for i in range(NSLOT)])

    def z_block(step):
        return lax.dynamic_index_in_dim(part_x, (z + step) % 4, 1, keepdims=False)

    from_z = shifts(z_block, "z", 4)
    part_z = add(z_block(0), *from_z).astype(BF)
    kept = lax.dynamic_index_in_dim(part_z, yhi, 0, keepdims=False)
    given = lax.dynamic_index_in_dim(part_z, 1 - yhi, 0, keepdims=False)
    from_y = [lax.ppermute(given if mask & 1 else kept, ("ylo", "yhi"), [(i, i ^ mask) for i in range(4)]) for mask in (1, 2, 3)]
    outs = receive(near, far, outs, (0, 1))
    from_y, outs = lax.optimization_barrier((from_y, outs))
    total = add(kept, *from_y).astype(BF)
    held = [total, *shifts(lambda step: total, "z", 4)]
    *outs, total = lax.optimization_barrier((*outs, total))
    outs = receive(near, far, outs, (2, 3))
    held, outs = lax.optimization_barrier((held, outs))


    held = jnp.stack(held)
    half = jnp.concatenate([lax.dynamic_index_in_dim(held, (z - b) % 4, 0, keepdims=False) for b in range(4)], axis=0)
    twin = swap(half, "core", 2, 1)
    first = jnp.where(core == 0, half, twin)
    second = jnp.where(core == 0, twin, half)
    return (*outs, jnp.concatenate([first, second], axis=0).astype(F32))


def solution(mesh):
    fine = Mesh(mesh.devices.reshape(2, 4, 2, 2, 4), FINE)
    rows = P(FINE, None)
    return jax.shard_map(
        per_device,
        mesh=fine,
        in_specs=(rows,) * 9 + (P(DP, ("yhi", "x"), None, None),),
        out_specs=(rows, rows, rows, rows, P(("yhi", "x"), None)),
        check_vma=False,
    )
```
